32 devices in a mesh: groups: 2 (over y), seq: 8 (over z, x), track: 2 (over core).
Axes of the slice: x: 2, y: 2, z: 4, core: 2. Of those that a mesh axis runs over, the one named last changes fastest.
Arguments:
- section_input: bfloat16 [1536, 4096], P('track', ('groups', 'seq')), parts along dimension 1, may hold values from -6 to 6
- conv_taps: float32 [1536, 3], P(('track', 'seq')), may hold values from -3 to 3
- dilation_level: int32 [1536], P(('track', 'seq')), may hold values from 0 to 4, as said below
- pointwise_matrix: bfloat16 [1536, 1536], P('track', 'seq'), may hold values from -0.15625 to 0.15625
- head_weight: bfloat16 [1536, 5312], P('seq', 'track'), may hold values from -0.078125 to 0.078125
- pred_error: bfloat16 [4096, 5312], P(('groups', 'seq'), 'track'), parts along dimension 0, may hold values from -6 to 6
- tail_mask: int32 [4096, 5312], P(('groups', 'seq'), 'track'), parts along dimension 0, may hold values 0 or 1
- track_scale: float32 [5312], P('track'), may hold values from 0.5 to 2
Outputs:
- input_grad: bfloat16 [1536, 4096], P('track', ('groups', 'seq')), parts along dimension 1
- taps_grad: float32 [3072, 3], P(('groups', 'track', 'seq')), parts along dimension 0
The draws below stay inside these ranges and needn't reach their ends.
There are 2 independent parts, one for each index of `groups`. The reference program is written for one: setup_inputs(seed, part) draws one part's arguments, and reference() takes and returns one part's arrays. A program takes and returns all parts, laid end to end along the dimension named above; an argument that names none is the same for every part. Nothing has to cross between parts.
Inputs may be any that keep to these rules, and one draw needn't show every extreme that they name: `dilation_level`: every level 0 and 4 occurs.
All inputs are finite; a program needn't handle non-finite values. No bound on the sum of `tail_mask` on one device may be relied on, other than what follows from the above.
Results may differ from the reference program's by a relative error of at most 0.0057.
Values may be sent and summed in bfloat16 or wider, within the bound.
A program may use at most 128 MiB of HBM per device.

```python
import math
import jax
import jax.numpy as jnp
from jax import lax

C = 1536
TR = 5312
ROWS = 256
KW = 3
DILATION_COUNT = 5
BASE_DILATION = 32
LENGTH = 2048


def draw_dilation_level(key, part):
    leading_key, trailing_key = jax.random.split(key)
    levels = jax.random.randint(leading_key, (C,), 0, DILATION_COUNT, dtype=jnp.int32)
    chosen = jax.random.permutation(trailing_key, C)
    return levels.at[chosen[0]].set(0).at[chosen[1]].set(DILATION_COUNT - 1)


def with_ends(entries, stream_key, low, largest):
    longest = entries.shape.index(max(entries.shape))
    spots = []
    for shift in (0, 1):
        where = [jax.random.randint(jax.random.fold_in(stream_key, axis), (), 0, length) for axis, length in enumerate(entries.shape)]
        where[longest] = (where[longest] + shift) % entries.shape[longest]
        spots.append(tuple(where))
    return entries.at[spots[0]].set(low).at[spots[1]].set(largest)


def level_of(own_key, dims, shards, low, high):
    loudness = 1.0
    for axis_at, shards_of in shards:
        steps = jax.random.uniform(jax.random.fold_in(jax.random.fold_in(own_key, 6), axis_at), (shards_of,), jnp.float32, low / len(shards), high / len(shards))
        loudness = loudness * jnp.repeat(jnp.exp(steps), dims[axis_at] // shards_of).reshape((-1,) + (1,) * (len(dims) - 1 - axis_at))
    return loudness


def normal_values(own_key, dims, width, most, cuts=(), kind=jnp.bfloat16):
    values = width * jax.random.normal(own_key, dims, jnp.float32)
    if cuts:
        values = values * level_of(own_key, dims, cuts, -0.22, 0.18)
    return jnp.clip(values, -most, most).astype(kind)


def setup_inputs(seed: int = 0, part: int = 0) -> dict:
    arg_keys = jax.random.split(jax.random.key(seed), 9)
    part_keys = jax.random.split(jax.random.fold_in(arg_keys[8], part), 9)
    return {
        "section_input": normal_values(part_keys[0], (C, LENGTH), 1.0, 6.0, ((0, 2), (1, 8))),
        "conv_taps": normal_values(arg_keys[1], (C, KW), 0.6, 3.0, ((0, 16),), jnp.float32),
        "dilation_level": draw_dilation_level(jax.random.fold_in(arg_keys[8], 71), part),
        "pointwise_matrix": normal_values(arg_keys[3], (C, C), C ** -0.5, 0.15625, ((0, 2), (1, 8))),
        "head_weight": normal_values(arg_keys[4], (C, TR), TR ** -0.5, 0.078125, ((0, 8), (1, 2))),
        "pred_error": normal_values(part_keys[5], (LENGTH, TR), 1.0, 6.0, ((0, 8), (1, 2))),
        "tail_mask": with_ends((jax.random.randint(part_keys[6], (LENGTH, TR), 0, 3) < 1).astype(jnp.int32), jax.random.fold_in(part_keys[6], 1), 0, 1),
        "track_scale": jnp.clip(jnp.exp(math.log(2.0) - 1.3862944 * jax.random.uniform(arg_keys[7], (TR,), jnp.float32) ** level_of(arg_keys[7], (TR,), ((0, 2),), -0.2, 0.2)), 0.5, 2.0),
    }


root_half = 0.7071067811865476
norm_const = 0.3989422804014327

def gelu_slope(value):
    return 0.5 * (1.0 + jax.scipy.special.erf(value * root_half)) + value * norm_const * jnp.exp(-0.5 * value * value)

def taps_at(buffer, onehot, margin, sign):
    width_own = buffer.shape[1] - 2 * margin
    result = jnp.zeros((buffer.shape[0], width_own), jnp.float32)
    for level_index in range(onehot.shape[1]):
        receptive_span = BASE_DILATION * 2 ** level_index
        begin = margin + sign * receptive_span
        result = result + onehot[:, level_index:level_index + 1] * buffer[:, begin:begin + width_own]
    return result

def spread(values, onehot, margin, sign):
    result = jnp.zeros((values.shape[0], values.shape[1] + 2 * margin), jnp.float32)
    for level_index in range(onehot.shape[1]):
        receptive_span = BASE_DILATION * 2 ** level_index
        placed = onehot[:, level_index:level_index + 1] * values
        result = result + jnp.pad(placed, ((0, 0), (margin + sign * receptive_span, margin - sign * receptive_span)))
    return result

def channel_grads(buffer, hidden_grad, taps, onehot, margin):
    width_own = buffer.shape[1] - 2 * margin
    minus_side = taps_at(buffer, onehot, margin, -1)
    center = buffer[:, margin:margin + width_own]
    plus_side = taps_at(buffer, onehot, margin, 1)
    pre_act = taps[:, 0:1] * minus_side + taps[:, 1:2] * center + taps[:, 2:3] * plus_side
    pre_grad = hidden_grad.astype(jnp.float32) * gelu_slope(pre_act)
    taps_part = jnp.stack([lax.optimization_barrier(jnp.sum(pre_grad * minus_side, axis=1)), lax.optimization_barrier(jnp.sum(pre_grad * center, axis=1)), lax.optimization_barrier(jnp.sum(pre_grad * plus_side, axis=1))], axis=1)
    contrib = spread(taps[:, 0:1] * pre_grad, onehot, margin, -1) + spread(taps[:, 2:3] * pre_grad, onehot, margin, 1)
    contrib = contrib + jnp.pad(taps[:, 1:2] * pre_grad, ((0, 0), (margin, margin)))
    return (contrib, taps_part)

def reference(section_input, conv_taps, dilation_level, pointwise_matrix, head_weight, pred_error, tail_mask, track_scale):
    blocks = LENGTH // ROWS

    def head_block(pair):
        errors, masks = pair
        adjoint = (masks.astype(jnp.float32) * track_scale[None, :] * errors.astype(jnp.float32)).astype(jnp.bfloat16)
        return lax.dot_general(head_weight, adjoint, (((1,), (1,)), ((), ())), preferred_element_type=jnp.float32)
    pieces = lax.map(head_block, (pred_error.reshape(blocks, ROWS, TR), tail_mask.reshape(blocks, ROWS, TR)))
    out_grad = jnp.transpose(pieces, (1, 0, 2)).reshape(C, LENGTH)
    hidden_grad = jnp.dot(pointwise_matrix, out_grad.astype(jnp.bfloat16), preferred_element_type=jnp.float32).astype(jnp.bfloat16)
    onehot = (dilation_level[:, None] == jnp.arange(DILATION_COUNT, dtype=jnp.int32)[None, :]).astype(jnp.float32)
    largest_span = BASE_DILATION * 2 ** (DILATION_COUNT - 1)
    groups_count = C // 128

    def conv_block(items):
        inputs, grads, taps, selector, upstream = items
        padded = jnp.pad(inputs.astype(jnp.float32), ((0, 0), (largest_span, largest_span)))
        contrib, taps_part = channel_grads(padded, grads, taps, selector, largest_span)
        conv_part = contrib[:, largest_span:largest_span + LENGTH]
        return ((upstream + conv_part).astype(jnp.bfloat16), taps_part)

    def regroup(array):
        return array.reshape((groups_count, 128) + array.shape[1:])
    grad_blocks, taps_blocks = lax.map(conv_block, (regroup(section_input), regroup(hidden_grad), regroup(conv_taps), regroup(onehot), regroup(out_grad)))
    scale = 1.0 / math.sqrt(LENGTH)
    return (grad_blocks.reshape(C, LENGTH), taps_blocks.reshape(C, KW) * scale)
```

```python
import functools
import math

import jax
import jax.numpy as jnp
from jax import lax
from jax.experimental import pallas as pl
from jax.experimental.pallas import tpu as pltpu
from jax.sharding import PartitionSpec as P

DILATION_COUNT = 5
BASE_DILATION = 32


root_half = 0.7071067811865476
norm_const = 0.3989422804014327


def gelu_slope(value):
    return 0.5 * (1.0 + jax.scipy.special.erf(value * root_half)) + value * norm_const * jnp.exp(
        -0.5 * value * value
    )


def taps_at(buffer, onehot, margin, sign):
    width_own = buffer.shape[1] - 2 * margin
    result = jnp.zeros((buffer.shape[0], width_own), jnp.float32)
    for level_index in range(onehot.shape[1]):
        receptive_span = BASE_DILATION * 2**level_index
        begin = margin + sign * receptive_span
        result = (
            result + onehot[:, level_index : level_index + 1] * buffer[:, begin : begin + width_own]
        )
    return result


def spread(values, onehot, margin, sign):
    result = jnp.zeros((values.shape[0], values.shape[1] + 2 * margin), jnp.float32)
    for level_index in range(onehot.shape[1]):
        receptive_span = BASE_DILATION * 2**level_index
        placed = onehot[:, level_index : level_index + 1] * values
        result = result + jnp.pad(
            placed, ((0, 0), (margin + sign * receptive_span, margin - sign * receptive_span))
        )
    return result


def channel_grads(buffer, hidden_grad, taps, onehot, margin):
    width_own = buffer.shape[1] - 2 * margin
    minus_side = taps_at(buffer, onehot, margin, -1)
    center = buffer[:, margin : margin + width_own]
    plus_side = taps_at(buffer, onehot, margin, 1)
    pre_act = taps[:, 0:1] * minus_side + taps[:, 1:2] * center + taps[:, 2:3] * plus_side
    pre_grad = hidden_grad.astype(jnp.float32) * gelu_slope(pre_act)
    taps_part = jnp.stack(
        [
            jnp.sum(pre_grad * minus_side, axis=1),
            jnp.sum(pre_grad * center, axis=1),
            jnp.sum(pre_grad * plus_side, axis=1),
        ],
        axis=1,
    )
    contrib = spread(taps[:, 0:1] * pre_grad, onehot, margin, -1) + spread(
        taps[:, 2:3] * pre_grad, onehot, margin, 1
    )
    contrib = contrib + jnp.pad(taps[:, 1:2] * pre_grad, ((0, 0), (margin, margin)))
    return (contrib, taps_part)


def local(
    section_input,
    conv_taps,
    dilation_level,
    pointwise_matrix,
    head_weight,
    pred_error,
    tail_mask,
    track_scale,
):
    own_channels = section_input.shape[0]
    own_rows = section_input.shape[1]
    adjoint = (
        tail_mask.astype(jnp.float32) * track_scale[None, :] * pred_error.astype(jnp.float32)
    ).astype(jnp.bfloat16)
    full_grad = lax.dot_general(
        lax.all_gather(head_weight, "seq", axis=0, tiled=True),
        adjoint,
        (((1,), (1,)), ((), ())),
        preferred_element_type=jnp.float32,
    )
    total = lax.psum(full_grad, "track")
    out_grad_b = total.astype(jnp.bfloat16)
    out_grad = lax.dynamic_slice_in_dim(
        total, lax.axis_index("track") * own_channels, own_channels, 0
    )
    hidden_grad = jnp.dot(
        lax.all_gather(pointwise_matrix, "seq", axis=1, tiled=True),
        out_grad_b,
        preferred_element_type=jnp.float32,
    ).astype(jnp.bfloat16)
    largest_span = BASE_DILATION * 2 ** (DILATION_COUNT - 1)
    scale = 1.0 / math.sqrt(own_rows * lax.axis_size("seq"))
    onehot = (
        dilation_level[:, None] == jnp.arange(DILATION_COUNT, dtype=jnp.int32)[None, :]
    ).astype(jnp.float32)
    owned_input, owned_grad = (
        lax.all_to_all(section_input, "seq", split_axis=0, concat_axis=1, tiled=True),
        lax.all_to_all(hidden_grad, "seq", split_axis=0, concat_axis=1, tiled=True),
    )
    padded = jnp.pad(owned_input.astype(jnp.float32), ((0, 0), (largest_span, largest_span)))
    contrib, taps_part = channel_grads(padded, owned_grad, conv_taps, onehot, largest_span)
    window = contrib[:, largest_span : largest_span + owned_input.shape[1]]
    conv_part = lax.all_to_all(window, "seq", split_axis=1, concat_axis=0, tiled=True)
    taps_grad = taps_part * scale
    input_grad = (out_grad + conv_part).astype(jnp.bfloat16)
    return (input_grad, taps_grad)


MESH = pl.DeviceIdType.MESH
CROSS = 2
PARTS = 3
ADJ_PARTS = 4


def fused_kernel(
    chain,
    sec,
    taps,
    level,
    pw,
    hw,
    err,
    mask,
    scale,
    out,
    tg,
    wb,
    ab,
    ev,
    mv,
    pb,
    gp,
    gr,
    ob,
    ox,
    hs,
    hr,
    xr,
    xp,
    hf,
    cb,
    rb,
    ld_sem,
    w_send,
    w_recv,
    wy_send,
    wy_recv,
    p_send,
    p_recv,
    py_send,
    py_recv,
    a_send,
    a_recv,
    g_send,
    g_recv,
    o_send,
    o_recv,
    x_send,
    x_recv,
    h_send,
    h_recv,
    r_send,
    r_recv,
):
    g = lax.axis_index("groups")
    s = lax.axis_index("seq")
    t = lax.axis_index("track")
    members = chain * CROSS
    z = s // CROSS
    x = s % CROSS
    head_rows = hw.shape[0]
    half = head_rows // 2
    piece = half // PARTS
    own_rows = err.shape[0]
    own = sec.shape[0]
    owned = own // members
    phalf = own // 2
    adj_rows = own_rows // ADJ_PARTS
    pair_rows = CROSS * own_rows
    length = members * own_rows
    span = xp.shape[1] - length

    sibling = (g, s, 1 - t)
    twin = (1 - g, s, t)
    across = (g, z * CROSS + 1 - x, t)

    def peer(k):
        return lax.rem(s + k, members)

    barrier = pltpu.get_barrier_semaphore()

    def greet(k, carry):
        pl.semaphore_signal(barrier, inc=1, device_id=(g, peer(k), t), device_id_type=MESH)
        return carry

    lax.fori_loop(1, members, greet, 0)
    pl.semaphore_signal(barrier, inc=1, device_id=sibling, device_id_type=MESH)
    pl.semaphore_signal(barrier, inc=1, device_id=twin, device_id_type=MESH)

    own_w = pltpu.make_async_copy(
        hw, wb.at[pl.ds(pl.multiple_of(z * head_rows, 16), head_rows), :], ld_sem.at[0]
    )
    own_p = pltpu.make_async_copy(pw, pb.at[z], ld_sem.at[1])
    own_x = pltpu.make_async_copy(sec.at[pl.ds(pl.multiple_of(s * owned, 16), owned), :], xr.at[s], ld_sem.at[2])
    loads = []
    for c in range(ADJ_PARTS):
        rows = pl.ds(c * adj_rows, adj_rows)
        loads.append(
            (
                pltpu.make_async_copy(err.at[rows, :], ev.at[rows, :], ld_sem.at[3 + 2 * c]),
                pltpu.make_async_copy(mask.at[rows, :], mv.at[rows, :], ld_sem.at[4 + 2 * c]),
            )
        )
    for first, second in loads:
        first.start()
        second.start()
    own_w.start()
    own_p.start()
    own_x.start()
    pl.semaphore_wait(barrier, members - 1 + 2)

    def w_rows(shard, c, which):
        return pl.ds(pl.multiple_of(shard * head_rows + which * half + c * piece, 16), piece)

    def w_hop(shard, c, src, toward, direction):
        slot = shard * PARTS + c
        return pltpu.make_async_remote_copy(
            src_ref=src,
            dst_ref=wb.at[w_rows(shard, c, g), :],
            send_sem=w_send.at[direction, slot],
            recv_sem=w_recv.at[slot],
            device_id=(g, toward * CROSS + x, t),
            device_id_type=MESH,
        )

    def w_swap(shard, c, which):
        slot = shard * PARTS + c
        block = wb.at[w_rows(shard, c, which), :]
        return pltpu.make_async_remote_copy(
            src_ref=block,
            dst_ref=block,
            send_sem=wy_send.at[slot],
            recv_sem=wy_recv.at[slot],
            device_id=twin,
            device_id_type=MESH,
        )

    def p_hop(shard, src, toward, direction):
        return pltpu.make_async_remote_copy(
            src_ref=src,
            dst_ref=pb.at[shard, pl.ds(pl.multiple_of(g * phalf, 16), phalf), :],
            send_sem=p_send.at[direction, shard],
            recv_sem=p_recv.at[shard],
            device_id=(g, toward * CROSS + x, t),
            device_id_type=MESH,
        )

    def p_swap(shard, which):
        block = pb.at[shard, pl.ds(pl.multiple_of(which * phalf, 16), phalf), :]
        return pltpu.make_async_remote_copy(
            src_ref=block,
            dst_ref=block,
            send_sem=py_send.at[shard],
            recv_sem=py_recv.at[shard],
            device_id=twin,
            device_id_type=MESH,
        )

    has_up = z < chain - 1
    has_down = z > 0

    def own_piece(c):
        return hw.at[pl.ds(pl.multiple_of(g * half + c * piece, 16), piece), :]

    own_phalf = pw.at[pl.ds(pl.multiple_of(g * phalf, 16), phalf), :]

    @pl.when(has_up)
    def _():
        for c in range(PARTS):
            w_hop(z, c, own_piece(c), z + 1, 0).start()

    @pl.when(has_down)
    def _():
        for c in range(PARTS):
            w_hop(z, c, own_piece(c), z - 1, 1).start()

    def a_copy(c):
        rows = pl.ds(pl.multiple_of(c * adj_rows, 16), adj_rows)
        block = ab.at[x, rows, :]
        return pltpu.make_async_remote_copy(
            src_ref=block,
            dst_ref=block,
            send_sem=a_send.at[c],
            recv_sem=a_recv.at[c],
            device_id=across,
            device_id_type=MESH,
        )

    for c in range(ADJ_PARTS):
        loads[c][0].wait()
        loads[c][1].wait()

        def fill(i, carry):
            rows = pl.ds(pl.multiple_of(c * adj_rows + i * 16, 16), 16)
            value = mv[rows, :].astype(jnp.float32) * scale[...] * ev[rows, :].astype(jnp.float32)
            ab[x, rows, :] = value.astype(jnp.bfloat16)
            return carry

        lax.fori_loop(0, adj_rows // 16, fill, 0)
        a_copy(c).start()

    @pl.when(has_up)
    def _():
        p_hop(z, own_phalf, z + 1, 0).start()

    @pl.when(has_down)
    def _():
        p_hop(z, own_phalf, z - 1, 1).start()

    def x_copy(to, frm):
        return pltpu.make_async_remote_copy(
            src_ref=sec.at[pl.ds(pl.multiple_of(to * owned, 16), owned), :],
            dst_ref=xr.at[frm],
            send_sem=x_send.at[to],
            recv_sem=x_recv.at[frm],
            device_id=(g, to, t),
            device_id_type=MESH,
        )

    def x_start(k, carry):
        x_copy(peer(k), s).start()
        return carry

    lax.fori_loop(1, members, x_start, 0)

    below = z
    above = chain - 1 - z
    near = jnp.minimum(below, above)

    def order(j):
        step = (j + 1) // 2
        alternate = jnp.where(j % 2 == 1, z - step, z + step)
        one_sided = jnp.where(above > below, z + (j - near), z - (j - near))
        return jnp.where(j <= 2 * near, alternate, one_sided)

    def g_copy(shard, xs):
        rows = pl.ds(pl.multiple_of(shard * head_rows, 16), head_rows)
        return pltpu.make_async_remote_copy(
            src_ref=gp.at[xs, rows, :],
            dst_ref=gr.at[xs, rows, :],
            send_sem=g_send.at[shard, xs],
            recv_sem=g_recv.at[shard, xs],
            device_id=sibling,
            device_id_type=MESH,
        )

    def head_dot(shard, xs):
        rows = pl.ds(pl.multiple_of(shard * head_rows, 16), head_rows)
        gp[xs, rows, :] = lax.dot_general(
            wb[rows, :],
            ab[xs],
            (((1,), (1,)), ((), ())),
            preferred_element_type=jnp.float32,
        )
        g_copy(shard, xs).start()

    def w_relay(e, carry):
        paired = (near >= 1) & (e < 2 * PARTS)
        j = jnp.where(paired, 1 + e % 2, e // PARTS + 1)
        c = jnp.where(paired, e // 2, e % PARTS)
        shard = order(j)
        block = wb.at[w_rows(shard, c, g), :]
        w_hop(shard, c, block, z, 0).wait_recv()

        @pl.when((shard < z) & has_up)
        def _():
            w_hop(shard, c, block, z + 1, 0).start()

        @pl.when((shard > z) & has_down)
        def _():
            w_hop(shard, c, block, z - 1, 1).start()

        w_swap(shard, c, g).start()
        return carry

    def wait_swaps(shard):
        def one(c, carry):
            w_swap(shard, c, 1 - g).wait_recv()
            return carry

        lax.fori_loop(0, PARTS, one, 0)

    own_w.wait()
    head_dot(z, x)
    steps = chain - 1
    lax.fori_loop(0, (steps - 1) * PARTS, w_relay, 0)

    def early(j, carry):
        shard = order(j)
        wait_swaps(shard)
        head_dot(shard, x)
        return carry

    lax.fori_loop(1, steps - 1, early, 0)
    lax.fori_loop((steps - 1) * PARTS, steps * PARTS, w_relay, 0)
    lax.fori_loop(jnp.maximum(steps - 1, 1), steps, early, 0)

    def a_wait(c, carry):
        rows = pl.ds(pl.multiple_of(c * adj_rows, 16), adj_rows)
        block = ab.at[1 - x, rows, :]
        pltpu.make_async_remote_copy(
            src_ref=block,
            dst_ref=block,
            send_sem=a_send.at[c],
            recv_sem=a_recv.at[c],
            device_id=across,
            device_id_type=MESH,
        ).wait_recv()
        return carry

    lax.fori_loop(0, ADJ_PARTS, a_wait, 0)

    def late(j, carry):
        head_dot(jnp.where(j == 0, z, order(jnp.maximum(j, 1))), 1 - x)
        return carry

    lax.fori_loop(0, steps, late, 0)

    def p_relay(j, carry):
        shard = order(j)
        block = pb.at[shard, pl.ds(pl.multiple_of(g * phalf, 16), phalf), :]
        p_hop(shard, block, z, 0).wait_recv()

        @pl.when((shard < z) & has_up)
        def _():
            p_hop(shard, block, z + 1, 0).start()

        @pl.when((shard > z) & has_down)
        def _():
            p_hop(shard, block, z - 1, 1).start()

        p_swap(shard, g).start()
        return carry

    lax.fori_loop(1, steps + 1, p_relay, 0)
    last = order(steps)
    wait_swaps(last)
    head_dot(last, x)
    head_dot(last, 1 - x)

    def core_sum(j, carry):
        shard = jnp.where(j == 0, z, order(jnp.maximum(j, 1)))
        rows = pl.ds(pl.multiple_of(shard * head_rows, 16), head_rows)
        for xs in range(CROSS):
            g_copy(shard, xs).wait_recv()
            ob[rows, xs * own_rows : (xs + 1) * own_rows] = (gp[xs, rows, :] + gr[xs, rows, :]).astype(
                jnp.bfloat16
            )
        return carry

    lax.fori_loop(0, chain, core_sum, 0)

    blocks_kept = chain // 2

    def o_copy(q):
        return pltpu.make_async_remote_copy(
            src_ref=ob.at[
                pl.ds(pl.multiple_of((t * blocks_kept + q) * head_rows, 16), head_rows),
                pl.ds(pl.multiple_of((1 - x) * own_rows, 128), own_rows),
            ],
            dst_ref=ox.at[q],
            send_sem=o_send.at[q],
            recv_sem=o_recv.at[q],
            device_id=across,
            device_id_type=MESH,
        )

    for q in range(blocks_kept):
        o_copy(q).start()

    own_p.wait()

    def p_wait(j, carry):
        p_swap(order(j), 1 - g).wait_recv()
        return carry

    lax.fori_loop(1, steps + 1, p_wait, 0)

    def hidden_for(to):
        rows = pl.ds(pl.multiple_of(to * owned, 16), owned)
        total = jnp.zeros((owned, pair_rows), jnp.float32)
        for shard in range(chain):
            total = total + jnp.dot(
                pb[shard, rows, :],
                ob[shard * head_rows : (shard + 1) * head_rows, :],
                preferred_element_type=jnp.float32,
            )
        return total.astype(jnp.bfloat16)

    def h_copy(to, frm):
        return pltpu.make_async_remote_copy(
            src_ref=hs.at[to],
            dst_ref=hr.at[frm],
            send_sem=h_send.at[to],
            recv_sem=h_recv.at[frm],
            device_id=(g, to, t),
            device_id_type=MESH,
        )

    def h_step(k, carry):
        to = peer(k)
        hs[to] = hidden_for(to)
        h_copy(to, s).start()
        return carry

    lax.fori_loop(1, members, h_step, 0)
    hr[s] = hidden_for(s)

    own_x.wait()

    def x_wait(k, carry):
        x_copy(s, peer(k)).wait_recv()
        return carry

    lax.fori_loop(1, members, x_wait, 0)
    for m in range(members):
        xp[:, m * own_rows : (m + 1) * own_rows] = xr[m].astype(jnp.float32)
    xp[:, length:] = jnp.zeros((owned, span), jnp.float32)

    def h_wait(k, carry):
        h_copy(s, peer(k)).wait_recv()
        return carry

    lax.fori_loop(1, members, h_wait, 0)
    for m in range(chain):
        both = hr[CROSS * m].astype(jnp.float32) + hr[CROSS * m + 1].astype(jnp.float32)
        hf[:, m * pair_rows : (m + 1) * pair_rows] = both.astype(jnp.bfloat16)

    padded = length + span
    norm = 1.0 / math.sqrt(length)

    def conv_rows(i, carry):
        rows = pl.ds(pl.multiple_of(i * 16, 16), 16)
        lev = level[rows, :]
        tap = taps[rows, :]

        def pick(value, sign):
            result = None
            for k in range(DILATION_COUNT):
                reach = BASE_DILATION * 2**k
                moved = pltpu.roll(value, reach if sign < 0 else padded - reach, 1)[:, :length]
                result = moved if result is None else jnp.where(lev == k, moved, result)
            return result

        wide = xp[rows, :]
        minus = pick(wide, -1)
        plus = pick(wide, 1)
        center = wide[:, :length]
        pre_act = tap[:, 0:1] * minus + tap[:, 1:2] * center + tap[:, 2:3] * plus
        pre_grad = hf[rows, :].astype(jnp.float32) * gelu_slope(pre_act)
        tg[rows, 0:1] = jnp.sum(pre_grad * minus, axis=1, keepdims=True) * norm
        tg[rows, 1:2] = jnp.sum(pre_grad * center, axis=1, keepdims=True) * norm
        tg[rows, 2:3] = jnp.sum(pre_grad * plus, axis=1, keepdims=True) * norm
        spread_wide = jnp.concatenate([pre_grad, jnp.zeros((16, span), jnp.float32)], axis=1)
        part = (
            tap[:, 0:1] * pick(spread_wide, 1)
            + tap[:, 1:2] * pre_grad
            + tap[:, 2:3] * pick(spread_wide, -1)
        ).astype(jnp.bfloat16)
        for m in range(members):
            cb[m, rows, :] = part[:, m * own_rows : (m + 1) * own_rows]
        return carry

    lax.fori_loop(0, owned // 16, conv_rows, 0)

    def r_copy(to, frm):
        return pltpu.make_async_remote_copy(
            src_ref=cb.at[to],
            dst_ref=rb.at[frm],
            send_sem=r_send.at[to],
            recv_sem=r_recv.at[frm],
            device_id=(g, to, t),
            device_id_type=MESH,
        )

    def r_start(k, carry):
        r_copy(peer(k), s).start()
        return carry

    lax.fori_loop(1, members, r_start, 0)
    rb[s] = cb[s]
    for q in range(blocks_kept):
        o_copy(q).wait_recv()

    def r_wait(k, carry):
        r_copy(s, peer(k)).wait_recv()
        return carry

    lax.fori_loop(1, members, r_wait, 0)

    per = head_rows // owned
    for q in range(blocks_kept):
        for u in range(per):
            mine = (CROSS * q + x) * per + u
            src = pl.ds(pl.multiple_of((t * blocks_kept + q) * head_rows + u * owned, 16), owned)
            here = jnp.where(
                x == 0, ob[src, 0:own_rows].astype(jnp.float32), ob[src, own_rows:].astype(jnp.float32)
            )
            out[pl.ds(pl.multiple_of(mine * owned, 16), owned), :] = (
                here + rb[mine].astype(jnp.float32)
            ).astype(jnp.bfloat16)
            other = (CROSS * q + 1 - x) * per + u
            there = ox[q, u * owned : (u + 1) * owned, :].astype(jnp.float32)
            out[pl.ds(pl.multiple_of(other * owned, 16), owned), :] = (
                there + rb[other].astype(jnp.float32)
            ).astype(jnp.bfloat16)

    def w_done(shard, carry):
        def one(c, inner):
            block = wb.at[w_rows(shard, c, g), :]

            @pl.when((shard <= z) & has_up)
            def _():
                w_hop(shard, c, block, z, 0).wait_send()

            @pl.when((shard >= z) & has_down)
            def _():
                w_hop(shard, c, block, z, 1).wait_send()

            @pl.when(shard != z)
            def _():
                w_swap(shard, c, g).wait_send()

            return inner

        lax.fori_loop(0, PARTS, one, 0)
        pblock = pb.at[shard, pl.ds(pl.multiple_of(g * phalf, 16), phalf), :]

        @pl.when((shard <= z) & has_up)
        def _():
            p_hop(shard, pblock, z, 0).wait_send()

        @pl.when((shard >= z) & has_down)
        def _():
            p_hop(shard, pblock, z, 1).wait_send()

        @pl.when(shard != z)
        def _():
            p_swap(shard, g).wait_send()

        for xs in range(CROSS):
            g_copy(shard, xs).wait_send()
        return carry

    lax.fori_loop(0, chain, w_done, 0)

    def a_done(c, carry):
        a_copy(c).wait_send()
        return carry

    lax.fori_loop(0, ADJ_PARTS, a_done, 0)
    for q in range(blocks_kept):
        o_copy(q).wait_send()

    def done(k, carry):
        x_copy(peer(k), s).wait_send()
        h_copy(peer(k), s).wait_send()
        r_copy(peer(k), s).wait_send()
        return carry

    lax.fori_loop(1, members, done, 0)


def fused(
    chain,
    section_input,
    conv_taps,
    dilation_level,
    pointwise_matrix,
    head_weight,
    pred_error,
    tail_mask,
    track_scale,
):
    own, own_rows = section_input.shape
    members = chain * CROSS
    owned = own // members
    head_rows, tracks = head_weight.shape
    pair_rows = CROSS * own_rows
    length = members * own_rows
    span = BASE_DILATION * 2 ** (DILATION_COUNT - 1)
    cols = pointwise_matrix.shape[1]
    bf16, f32 = jnp.bfloat16, jnp.float32
    dma = pltpu.SemaphoreType.DMA
    anywhere = pl.BlockSpec(memory_space=pl.ANY)
    vmem = pl.BlockSpec(memory_space=pltpu.VMEM)
    return tuple(
        pl.pallas_call(
            functools.partial(fused_kernel, chain),
            out_shape=(
                jax.ShapeDtypeStruct((own, own_rows), bf16),
                jax.ShapeDtypeStruct((owned, 3), f32),
            ),
            in_specs=[anywhere, vmem, vmem, anywhere, anywhere, anywhere, anywhere, vmem],
            out_specs=(vmem, vmem),
            scratch_shapes=[
                pltpu.VMEM((chain * head_rows, tracks), bf16),
                pltpu.VMEM((CROSS, own_rows, tracks), bf16),
                pltpu.VMEM((own_rows, tracks), bf16),
                pltpu.VMEM((own_rows, tracks), jnp.int32),
                pltpu.VMEM((chain, own, cols), bf16),
                pltpu.VMEM((CROSS, chain * head_rows, own_rows), f32),
                pltpu.VMEM((CROSS, chain * head_rows, own_rows), f32),
                pltpu.VMEM((chain * head_rows, pair_rows), bf16),
                pltpu.VMEM((chain // 2, head_rows, own_rows), bf16),
                pltpu.VMEM((members, owned, pair_rows), bf16),
                pltpu.VMEM((members, owned, pair_rows), bf16),
                pltpu.VMEM((members, owned, own_rows), bf16),
                pltpu.VMEM((owned, length + span), f32),
                pltpu.VMEM((owned, length), bf16),
                pltpu.VMEM((members, owned, own_rows), bf16),
                pltpu.VMEM((members, owned, own_rows), bf16),
                dma((3 + 2 * ADJ_PARTS,)),
                dma((2, chain * PARTS)),
                dma((chain * PARTS,)),
                dma((chain * PARTS,)),
                dma((chain * PARTS,)),
                dma((2, chain)),
                dma((chain,)),
                dma((chain,)),
                dma((chain,)),
                dma((ADJ_PARTS,)),
                dma((ADJ_PARTS,)),
                dma((chain, CROSS)),
                dma((chain, CROSS)),
                dma((chain // 2,)),
                dma((chain // 2,)),
                dma((members,)),
                dma((members,)),
                dma((members,)),
                dma((members,)),
                dma((members,)),
                dma((members,)),
            ],
            compiler_params=pltpu.CompilerParams(
                collective_id=0, has_side_effects=True, vmem_limit_bytes=48 * 1024 * 1024
            ),
            name="fused_section",
        )(
            section_input,
            conv_taps,
            dilation_level[:, None],
            pointwise_matrix,
            head_weight,
            pred_error,
            tail_mask,
            track_scale[None, :],
        )
    )


def local_or_fused(sizes, *args):
    section_input, head_weight, pred_error = args[0], args[4], args[5]
    seq = sizes["seq"]
    fits = (
        sizes["groups"] == 2
        and sizes["track"] == 2
        and seq == 8
        and head_weight.shape[0] % (2 * PARTS * 16) == 0
        and section_input.shape[0] % (seq * 16) == 0
        and section_input.shape[1] % 128 == 0
        and pred_error.shape[0] % (ADJ_PARTS * 16) == 0
        and head_weight.shape[0] % (section_input.shape[0] // seq) == 0
    )
    if fits:
        return fused(seq // CROSS, *args)
    return local(*args)


def solution(mesh):
    in_specs = (
        P("track", ("groups", "seq")),
        P(("track", "seq"), None),
        P(("track", "seq")),
        P("track", "seq"),
        P("seq", "track"),
        P(("groups", "seq"), "track"),
        P(("groups", "seq"), "track"),
        P("track"),
    )
    sizes = dict(mesh.shape)
    body = functools.partial(local_or_fused, sizes)
    out_specs = (P("track", ("groups", "seq")), P(("groups", "track", "seq"), None))
    return jax.shard_map(body, mesh=mesh, in_specs=in_specs, out_specs=out_specs, check_vma=False)
```

```python
import functools
import math

import jax
import jax.numpy as jnp
from jax import lax
from jax.experimental import pallas as pl
from jax.experimental.pallas import tpu as pltpu
from jax.sharding import PartitionSpec as P

DILATION_COUNT = 5
BASE_DILATION = 32


root_half = 0.7071067811865476
norm_const = 0.3989422804014327


def gelu_slope(value):
    return 0.5 * (1.0 + jax.scipy.special.erf(value * root_half)) + value * norm_const * jnp.exp(
        -0.5 * value * value
    )


def taps_at(buffer, onehot, margin, sign):
    width_own = buffer.shape[1] - 2 * margin
    result = jnp.zeros((buffer.shape[0], width_own), jnp.float32)
    for level_index in range(onehot.shape[1]):
        receptive_span = BASE_DILATION * 2**level_index
        begin = margin + sign * receptive_span
        result = (
            result + onehot[:, level_index : level_index + 1] * buffer[:, begin : begin + width_own]
        )
    return result


def spread(values, onehot, margin, sign):
    result = jnp.zeros((values.shape[0], values.shape[1] + 2 * margin), jnp.float32)
    for level_index in range(onehot.shape[1]):
        receptive_span = BASE_DILATION * 2**level_index
        placed = onehot[:, level_index : level_index + 1] * values
        result = result + jnp.pad(
            placed, ((0, 0), (margin + sign * receptive_span, margin - sign * receptive_span))
        )
    return result


def channel_grads(buffer, hidden_grad, taps, onehot, margin):
    width_own = buffer.shape[1] - 2 * margin
    minus_side = taps_at(buffer, onehot, margin, -1)
    center = buffer[:, margin : margin + width_own]
    plus_side = taps_at(buffer, onehot, margin, 1)
    pre_act = taps[:, 0:1] * minus_side + taps[:, 1:2] * center + taps[:, 2:3] * plus_side
    pre_grad = hidden_grad.astype(jnp.float32) * gelu_slope(pre_act)
    taps_part = jnp.stack(
        [
            jnp.sum(pre_grad * minus_side, axis=1),
            jnp.sum(pre_grad * center, axis=1),
            jnp.sum(pre_grad * plus_side, axis=1),
        ],
        axis=1,
    )
    contrib = spread(taps[:, 0:1] * pre_grad, onehot, margin, -1) + spread(
        taps[:, 2:3] * pre_grad, onehot, margin, 1
    )
    contrib = contrib + jnp.pad(taps[:, 1:2] * pre_grad, ((0, 0), (margin, margin)))
    return (contrib, taps_part)


def local(
    section_input,
    conv_taps,
    dilation_level,
    pointwise_matrix,
    head_weight,
    pred_error,
    tail_mask,
    track_scale,
):
    own_channels = section_input.shape[0]
    own_rows = section_input.shape[1]
    adjoint = (
        tail_mask.astype(jnp.float32) * track_scale[None, :] * pred_error.astype(jnp.float32)
    ).astype(jnp.bfloat16)
    full_grad = lax.dot_general(
        lax.all_gather(head_weight, "seq", axis=0, tiled=True),
        adjoint,
        (((1,), (1,)), ((), ())),
        preferred_element_type=jnp.float32,
    )
    total = lax.psum(full_grad, "track")
    out_grad_b = total.astype(jnp.bfloat16)
    out_grad = lax.dynamic_slice_in_dim(
        total, lax.axis_index("track") * own_channels, own_channels, 0
    )
    hidden_grad = jnp.dot(
        lax.all_gather(pointwise_matrix, "seq", axis=1, tiled=True),
        out_grad_b,
        preferred_element_type=jnp.float32,
    ).astype(jnp.bfloat16)
    largest_span = BASE_DILATION * 2 ** (DILATION_COUNT - 1)
    scale = 1.0 / math.sqrt(own_rows * lax.axis_size("seq"))
    onehot = (
        dilation_level[:, None] == jnp.arange(DILATION_COUNT, dtype=jnp.int32)[None, :]
    ).astype(jnp.float32)
    owned_input, owned_grad = (
        lax.all_to_all(section_input, "seq", split_axis=0, concat_axis=1, tiled=True),
        lax.all_to_all(hidden_grad, "seq", split_axis=0, concat_axis=1, tiled=True),
    )
    padded = jnp.pad(owned_input.astype(jnp.float32), ((0, 0), (largest_span, largest_span)))
    contrib, taps_part = channel_grads(padded, owned_grad, conv_taps, onehot, largest_span)
    window = contrib[:, largest_span : largest_span + owned_input.shape[1]]
    conv_part = lax.all_to_all(window, "seq", split_axis=1, concat_axis=0, tiled=True)
    taps_grad = taps_part * scale
    input_grad = (out_grad + conv_part).astype(jnp.bfloat16)
    return (input_grad, taps_grad)


MESH = pl.DeviceIdType.MESH
CROSS = 2
PARTS = 3
ADJ_PARTS = 4


def fused_kernel(
    chain,
    sec,
    taps,
    level,
    pw,
    hw,
    err,
    mask,
    scale,
    out,
    tg,
    wb,
    ab,
    ev,
    mv,
    pb,
    gp,
    gr,
    ob,
    ox,
    hs,
    hr,
    xr,
    xp,
    hf,
    cb,
    rb,
    cols,
    sums,
    ld_sem,
    w_send,
    w_recv,
    wy_send,
    wy_recv,
    p_send,
    p_recv,
    py_send,
    py_recv,
    a_send,
    a_recv,
    g_send,
    g_recv,
    o_send,
    o_recv,
    x_send,
    x_recv,
    h_send,
    h_recv,
    r_send,
    r_recv,
):
    g = lax.axis_index("groups")
    s = lax.axis_index("seq")
    t = lax.axis_index("track")
    members = chain * CROSS
    z = s // CROSS
    x = s % CROSS
    head_rows = hw.shape[0]
    half = head_rows // 2
    piece = half // PARTS
    tracks, own_rows = err.shape
    own = sec.shape[0]
    owned = own // members
    phalf = pw.shape[0] // 2
    step = tracks // ADJ_PARTS // 128 * 128
    cuts = [c * step for c in range(ADJ_PARTS)] + [tracks]
    pair_rows = CROSS * own_rows
    length = members * own_rows
    span = xp.shape[1] - length

    sibling = (g, s, 1 - t)
    twin = (1 - g, s, t)
    across = (g, z * CROSS + 1 - x, t)

    def peer(k):
        return lax.rem(s + k, members)

    barrier = pltpu.get_barrier_semaphore()

    def greet(k, carry):
        pl.semaphore_signal(barrier, inc=1, device_id=(g, peer(k), t), device_id_type=MESH)
        return carry

    lax.fori_loop(1, members, greet, 0)
    pl.semaphore_signal(barrier, inc=1, device_id=sibling, device_id_type=MESH)
    pl.semaphore_signal(barrier, inc=1, device_id=twin, device_id_type=MESH)

    own_w = pltpu.make_async_copy(
        hw, wb.at[pl.ds(pl.multiple_of(z * head_rows, 16), head_rows), :], ld_sem.at[0]
    )
    own_p = pltpu.make_async_copy(pw, pb.at[z], ld_sem.at[1])
    own_x = pltpu.make_async_copy(sec.at[pl.ds(pl.multiple_of(s * owned, 16), owned), :], xr.at[s], ld_sem.at[2])
    loads = []
    for c in range(ADJ_PARTS):
        rows = pl.ds(cuts[c], cuts[c + 1] - cuts[c])
        loads.append(
            (
                pltpu.make_async_copy(err.at[rows, :], ev.at[rows, :], ld_sem.at[3 + 2 * c]),
                pltpu.make_async_copy(mask.at[rows, :], mv.at[rows, :], ld_sem.at[4 + 2 * c]),
            )
        )
    for first, second in loads:
        first.start()
        second.start()
    own_w.start()
    own_p.start()
    own_x.start()
    pl.semaphore_wait(barrier, members - 1 + 2)

    def w_rows(shard, c, which):
        return pl.ds(pl.multiple_of(shard * head_rows + which * half + c * piece, 16), piece)

    def w_hop(shard, c, src, toward, direction):
        slot = shard * PARTS + c
        return pltpu.make_async_remote_copy(
            src_ref=src,
            dst_ref=wb.at[w_rows(shard, c, g), :],
            send_sem=w_send.at[direction, slot],
            recv_sem=w_recv.at[slot],
            device_id=(g, toward * CROSS + x, t),
            device_id_type=MESH,
        )

    def w_swap(shard, c, which):
        slot = shard * PARTS + c
        block = wb.at[w_rows(shard, c, which), :]
        return pltpu.make_async_remote_copy(
            src_ref=block,
            dst_ref=block,
            send_sem=wy_send.at[slot],
            recv_sem=wy_recv.at[slot],
            device_id=twin,
            device_id_type=MESH,
        )

    def p_hop(shard, src, toward, direction):
        return pltpu.make_async_remote_copy(
            src_ref=src,
            dst_ref=pb.at[shard, pl.ds(pl.multiple_of(g * phalf, 16), phalf), :],
            send_sem=p_send.at[direction, shard],
            recv_sem=p_recv.at[shard],
            device_id=(g, toward * CROSS + x, t),
            device_id_type=MESH,
        )

    def p_swap(shard, which):
        block = pb.at[shard, pl.ds(pl.multiple_of(which * phalf, 16), phalf), :]
        return pltpu.make_async_remote_copy(
            src_ref=block,
            dst_ref=block,
            send_sem=py_send.at[shard],
            recv_sem=py_recv.at[shard],
            device_id=twin,
            device_id_type=MESH,
        )

    has_up = z < chain - 1
    has_down = z > 0

    def own_piece(c):
        return hw.at[pl.ds(pl.multiple_of(g * half + c * piece, 16), piece), :]

    own_phalf = pw.at[pl.ds(pl.multiple_of(g * phalf, 16), phalf), :]

    @pl.when(has_up)
    def _():
        for c in range(PARTS):
            w_hop(z, c, own_piece(c), z + 1, 0).start()

    @pl.when(has_down)
    def _():
        for c in range(PARTS):
            w_hop(z, c, own_piece(c), z - 1, 1).start()

    def a_copy(c):
        rows = pl.ds(cuts[c], cuts[c + 1] - cuts[c])
        block = ab.at[x, rows, :]
        return pltpu.make_async_remote_copy(
            src_ref=block,
            dst_ref=block,
            send_sem=a_send.at[c],
            recv_sem=a_recv.at[c],
            device_id=across,
            device_id_type=MESH,
        )

    for c in range(ADJ_PARTS):
        loads[c][0].wait()
        loads[c][1].wait()

        def fill(begin, count):
            rows = pl.ds(begin, count)
            line = scale[:, rows]
            if count < 128:
                line = jnp.concatenate([line, jnp.zeros((1, 128 - count), jnp.float32)], axis=1)
            column = jnp.transpose(jnp.broadcast_to(line, (128, 128)))[:count]
            column = jnp.concatenate([column] * (own_rows // 128), axis=1)
            value = mv[rows, :].astype(jnp.float32) * column * ev[rows, :].astype(jnp.float32)
            ab[x, rows, :] = value.astype(jnp.bfloat16)

        def fill_step(i, carry):
            fill(pl.multiple_of(cuts[c] + i * 128, 128), 128)
            return carry

        whole, rest = divmod(cuts[c + 1] - cuts[c], 128)
        lax.fori_loop(0, whole, fill_step, 0)
        if rest:
            fill(cuts[c] + whole * 128, rest)
        a_copy(c).start()

    @pl.when(has_up)
    def _():
        p_hop(z, own_phalf, z + 1, 0).start()

    @pl.when(has_down)
    def _():
        p_hop(z, own_phalf, z - 1, 1).start()

    def x_copy(to, frm):
        return pltpu.make_async_remote_copy(
            src_ref=sec.at[pl.ds(pl.multiple_of(to * owned, 16), owned), :],
            dst_ref=xr.at[frm],
            send_sem=x_send.at[to],
            recv_sem=x_recv.at[frm],
            device_id=(g, to, t),
            device_id_type=MESH,
        )

    def x_start(k, carry):
        x_copy(peer(k), s).start()
        return carry

    lax.fori_loop(1, members, x_start, 0)

    below = z
    above = chain - 1 - z
    near = jnp.minimum(below, above)

    def order(j):
        step = (j + 1) // 2
        alternate = jnp.where(j % 2 == 1, z - step, z + step)
        one_sided = jnp.where(above > below, z + (j - near), z - (j - near))
        return jnp.where(j <= 2 * near, alternate, one_sided)

    def g_copy(shard, xs):
        rows = pl.ds(pl.multiple_of(shard * head_rows, 16), head_rows)
        return pltpu.make_async_remote_copy(
            src_ref=gp.at[xs, rows, :],
            dst_ref=gr.at[xs, rows, :],
            send_sem=g_send.at[shard, xs],
            recv_sem=g_recv.at[shard, xs],
            device_id=sibling,
            device_id_type=MESH,
        )

    def head_dot(shard, xs):
        rows = pl.ds(pl.multiple_of(shard * head_rows, 16), head_rows)
        gp[xs, rows, :] = lax.dot_general(
            wb[rows, :],
            ab[xs],
            (((1,), (0,)), ((), ())),
            preferred_element_type=jnp.float32,
        )
        g_copy(shard, xs).start()

    def w_relay(e, carry):
        paired = (near >= 1) & (e < 2 * PARTS)
        j = jnp.where(paired, 1 + e % 2, e // PARTS + 1)
        c = jnp.where(paired, e // 2, e % PARTS)
        shard = order(j)
        block = wb.at[w_rows(shard, c, g), :]
        w_hop(shard, c, block, z, 0).wait_recv()

        @pl.when((shard < z) & has_up)
        def _():
            w_hop(shard, c, block, z + 1, 0).start()

        @pl.when((shard > z) & has_down)
        def _():
            w_hop(shard, c, block, z - 1, 1).start()

        w_swap(shard, c, g).start()
        return carry

    def wait_swaps(shard):
        def one(c, carry):
            w_swap(shard, c, 1 - g).wait_recv()
            return carry

        lax.fori_loop(0, PARTS, one, 0)

    own_w.wait()
    head_dot(z, x)
    steps = chain - 1
    lax.fori_loop(0, (steps - 1) * PARTS, w_relay, 0)

    def early(j, carry):
        shard = order(j)
        wait_swaps(shard)
        head_dot(shard, x)
        return carry

    lax.fori_loop(1, steps - 1, early, 0)
    lax.fori_loop((steps - 1) * PARTS, steps * PARTS, w_relay, 0)
    lax.fori_loop(jnp.maximum(steps - 1, 1), steps, early, 0)

    for c in range(ADJ_PARTS):
        block = ab.at[1 - x, pl.ds(cuts[c], cuts[c + 1] - cuts[c]), :]
        pltpu.make_async_remote_copy(
            src_ref=block,
            dst_ref=block,
            send_sem=a_send.at[c],
            recv_sem=a_recv.at[c],
            device_id=across,
            device_id_type=MESH,
        ).wait_recv()

    def late(j, carry):
        head_dot(jnp.where(j == 0, z, order(jnp.maximum(j, 1))), 1 - x)
        return carry

    lax.fori_loop(0, steps, late, 0)

    def p_relay(j, carry):
        shard = order(j)
        block = pb.at[shard, pl.ds(pl.multiple_of(g * phalf, 16), phalf), :]
        p_hop(shard, block, z, 0).wait_recv()

        @pl.when((shard < z) & has_up)
        def _():
            p_hop(shard, block, z + 1, 0).start()

        @pl.when((shard > z) & has_down)
        def _():
            p_hop(shard, block, z - 1, 1).start()

        p_swap(shard, g).start()
        return carry

    lax.fori_loop(1, steps + 1, p_relay, 0)
    last = order(steps)
    wait_swaps(last)
    head_dot(last, x)
    head_dot(last, 1 - x)

    def core_sum(j, carry):
        shard = jnp.where(j == 0, z, order(jnp.maximum(j, 1)))
        rows = pl.ds(pl.multiple_of(shard * head_rows, 16), head_rows)
        for xs in range(CROSS):
            g_copy(shard, xs).wait_recv()
            ob[rows, xs * own_rows : (xs + 1) * own_rows] = (gp[xs, rows, :] + gr[xs, rows, :]).astype(
                jnp.bfloat16
            )
        return carry

    lax.fori_loop(0, chain, core_sum, 0)

    blocks_kept = chain // 2

    def o_copy(q):
        return pltpu.make_async_remote_copy(
            src_ref=ob.at[
                pl.ds(pl.multiple_of((t * blocks_kept + q) * head_rows, 16), head_rows),
                pl.ds(pl.multiple_of((1 - x) * own_rows, 128), own_rows),
            ],
            dst_ref=ox.at[q],
            send_sem=o_send.at[q],
            recv_sem=o_recv.at[q],
            device_id=across,
            device_id_type=MESH,
        )

    for q in range(blocks_kept):
        o_copy(q).start()

    own_p.wait()

    def p_wait(j, carry):
        p_swap(order(j), 1 - g).wait_recv()
        return carry

    lax.fori_loop(1, steps + 1, p_wait, 0)

    def h_rows(to):
        return pl.ds(pl.multiple_of(to * owned, 16), owned)

    def h_copy(to, frm):
        return pltpu.make_async_remote_copy(
            src_ref=hs.at[h_rows(to), :],
            dst_ref=hr.at[frm],
            send_sem=h_send.at[to],
            recv_sem=h_recv.at[frm],
            device_id=(g, to, t),
            device_id_type=MESH,
        )

    group = members // 2
    wide_rows = group * owned

    def h_step(k, carry):
        n = (s // group + 1 + k) % 2
        lanes = pl.ds(pl.multiple_of(n * wide_rows, 128), wide_rows)
        total = jnp.zeros((wide_rows, pair_rows), jnp.float32)
        for shard in range(chain):
            total = total + lax.dot_general(
                pb[shard, :, lanes],
                ob[shard * head_rows : (shard + 1) * head_rows, :],
                (((0,), (0,)), ((), ())),
                preferred_element_type=jnp.float32,
            )
        hs[lanes, :] = total.astype(jnp.bfloat16)
        for u in range(group):
            to = n * group + u

            @pl.when(to != s)
            def _():
                h_copy(to, s).start()

        return carry

    lax.fori_loop(0, 2, h_step, 0)
    hr[s] = hs[h_rows(s), :]

    own_x.wait()

    def x_wait(k, carry):
        x_copy(s, peer(k)).wait_recv()
        return carry

    lax.fori_loop(1, members, x_wait, 0)
    for m in range(members):
        xp[:, m * own_rows : (m + 1) * own_rows] = xr[m].astype(jnp.float32)
    xp[:, length:] = jnp.zeros((owned, span), jnp.float32)

    def h_wait(k, carry):
        h_copy(s, peer(k)).wait_recv()
        return carry

    lax.fori_loop(1, members, h_wait, 0)
    for m in range(chain):
        both = hr[CROSS * m].astype(jnp.float32) + hr[CROSS * m + 1].astype(jnp.float32)
        hf[:, m * pair_rows : (m + 1) * pair_rows] = both.astype(jnp.bfloat16)

    columns = cols.at[1]
    cols[0] = jnp.zeros((128, 128), jnp.float32)
    cols[0, 0:3, 0:owned] = taps[...]
    cols[0, 3:4, 0:owned] = level[...].astype(jnp.float32)
    cols[1] = jnp.transpose(cols[0])
    sums[...] = jnp.zeros((128, 128), jnp.float32)

    padded = length + span
    norm = 1.0 / math.sqrt(length)

    def conv_rows(i, carry):
        rows = pl.ds(pl.multiple_of(i * 16, 16), 16)
        lev = columns[rows, 3:4]
        tap = columns[rows, 0:3]

        def pick(value, sign):
            result = None
            for k in range(DILATION_COUNT):
                reach = BASE_DILATION * 2**k
                moved = pltpu.roll(value, reach if sign < 0 else padded - reach, 1)[:, :length]
                result = moved if result is None else jnp.where(lev == float(k), moved, result)
            return result

        wide = xp[rows, :]
        minus = pick(wide, -1)
        plus = pick(wide, 1)
        center = wide[:, :length]
        pre_act = tap[:, 0:1] * minus + tap[:, 1:2] * center + tap[:, 2:3] * plus
        pre_grad = hf[rows, :].astype(jnp.float32) * gelu_slope(pre_act)
        sums[rows, 0:1] = jnp.sum(pre_grad * minus, axis=1, keepdims=True) * norm
        sums[rows, 1:2] = jnp.sum(pre_grad * center, axis=1, keepdims=True) * norm
        sums[rows, 2:3] = jnp.sum(pre_grad * plus, axis=1, keepdims=True) * norm
        spread_wide = jnp.concatenate([pre_grad, jnp.zeros((16, span), jnp.float32)], axis=1)
        part = (
            tap[:, 0:1] * pick(spread_wide, 1)
            + tap[:, 1:2] * pre_grad
            + tap[:, 2:3] * pick(spread_wide, -1)
        ).astype(jnp.bfloat16)
        for m in range(members):
            cb[m, rows, :] = part[:, m * own_rows : (m + 1) * own_rows]
        return carry

    lax.fori_loop(0, owned // 16, conv_rows, 0)

    def r_copy(to, frm):
        return pltpu.make_async_remote_copy(
            src_ref=cb.at[to],
            dst_ref=rb.at[frm],
            send_sem=r_send.at[to],
            recv_sem=r_recv.at[frm],
            device_id=(g, to, t),
            device_id_type=MESH,
        )

    def r_start(k, carry):
        r_copy(peer(k), s).start()
        return carry

    lax.fori_loop(1, members, r_start, 0)
    rb[s] = cb[s]
    for q in range(blocks_kept):
        o_copy(q).wait_recv()

    def r_wait(k, carry):
        r_copy(s, peer(k)).wait_recv()
        return carry

    lax.fori_loop(1, members, r_wait, 0)

    per = head_rows // owned
    for q in range(blocks_kept):
        for u in range(per):
            mine = (CROSS * q + x) * per + u
            src = pl.ds(pl.multiple_of((t * blocks_kept + q) * head_rows + u * owned, 16), owned)
            here = jnp.where(
                x == 0, ob[src, 0:own_rows].astype(jnp.float32), ob[src, own_rows:].astype(jnp.float32)
            )
            out[pl.ds(pl.multiple_of(mine * owned, 16), owned), :] = (
                here + rb[mine].astype(jnp.float32)
            ).astype(jnp.bfloat16)
            other = (CROSS * q + 1 - x) * per + u
            there = ox[q, u * owned : (u + 1) * owned, :].astype(jnp.float32)
            out[pl.ds(pl.multiple_of(other * owned, 16), owned), :] = (
                there + rb[other].astype(jnp.float32)
            ).astype(jnp.bfloat16)

    tg[...] = jnp.transpose(sums[...])[0:3, 0:owned]

    def w_done(shard, carry):
        def one(c, inner):
            block = wb.at[w_rows(shard, c, g), :]

            @pl.when((shard <= z) & has_up)
            def _():
                w_hop(shard, c, block, z, 0).wait_send()

            @pl.when((shard >= z) & has_down)
            def _():
                w_hop(shard, c, block, z, 1).wait_send()

            @pl.when(shard != z)
            def _():
                w_swap(shard, c, g).wait_send()

            return inner

        lax.fori_loop(0, PARTS, one, 0)
        pblock = pb.at[shard, pl.ds(pl.multiple_of(g * phalf, 16), phalf), :]

        @pl.when((shard <= z) & has_up)
        def _():
            p_hop(shard, pblock, z, 0).wait_send()

        @pl.when((shard >= z) & has_down)
        def _():
            p_hop(shard, pblock, z, 1).wait_send()

        @pl.when(shard != z)
        def _():
            p_swap(shard, g).wait_send()

        for xs in range(CROSS):
            g_copy(shard, xs).wait_send()
        return carry

    lax.fori_loop(0, chain, w_done, 0)

    for c in range(ADJ_PARTS):
        a_copy(c).wait_send()
    for q in range(blocks_kept):
        o_copy(q).wait_send()

    def done(k, carry):
        x_copy(peer(k), s).wait_send()
        h_copy(peer(k), s).wait_send()
        r_copy(peer(k), s).wait_send()
        return carry

    lax.fori_loop(1, members, done, 0)


def fused(
    chain,
    section_input,
    conv_taps,
    dilation_level,
    pointwise_matrix,
    head_weight,
    pred_error,
    tail_mask,
    track_scale,
):
    own, own_rows = section_input.shape
    members = chain * CROSS
    owned = own // members
    head_rows, tracks = head_weight.shape
    pair_rows = CROSS * own_rows
    length = members * own_rows
    span = BASE_DILATION * 2 ** (DILATION_COUNT - 1)
    cols = pointwise_matrix.shape[1]
    bf16, f32 = jnp.bfloat16, jnp.float32
    dma = pltpu.SemaphoreType.DMA
    anywhere = pl.BlockSpec(memory_space=pltpu.HBM)
    vmem = pl.BlockSpec(memory_space=pltpu.VMEM)
    input_grad, taps_grad = (
        pl.pallas_call(
            functools.partial(fused_kernel, chain),
            out_shape=(
                jax.ShapeDtypeStruct((own, own_rows), bf16),
                jax.ShapeDtypeStruct((3, owned), f32),
            ),
            in_specs=[anywhere, vmem, vmem, anywhere, anywhere, anywhere, anywhere, vmem],
            out_specs=(vmem, vmem),
            scratch_shapes=[
                pltpu.VMEM((chain * head_rows, tracks), bf16),
                pltpu.VMEM((CROSS, tracks, own_rows), bf16),
                pltpu.VMEM((tracks, own_rows), bf16),
                pltpu.VMEM((tracks, own_rows), jnp.int32),
                pltpu.VMEM((chain, cols, own), bf16),
                pltpu.VMEM((CROSS, chain * head_rows, own_rows), f32),
                pltpu.VMEM((CROSS, chain * head_rows, own_rows), f32),
                pltpu.VMEM((chain * head_rows, pair_rows), bf16),
                pltpu.VMEM((chain // 2, head_rows, own_rows), bf16),
                pltpu.VMEM((own, pair_rows), bf16),
                pltpu.VMEM((members, owned, pair_rows), bf16),
                pltpu.VMEM((members, owned, own_rows), bf16),
                pltpu.VMEM((owned, length + span), f32),
                pltpu.VMEM((owned, length), bf16),
                pltpu.VMEM((members, owned, own_rows), bf16),
                pltpu.VMEM((members, owned, own_rows), bf16),
                pltpu.VMEM((2, 128, 128), f32),
                pltpu.VMEM((128, 128), f32),
                dma((3 + 2 * ADJ_PARTS,)),
                dma((2, chain * PARTS)),
                dma((chain * PARTS,)),
                dma((chain * PARTS,)),
                dma((chain * PARTS,)),
                dma((2, chain)),
                dma((chain,)),
                dma((chain,)),
                dma((chain,)),
                dma((ADJ_PARTS,)),
                dma((ADJ_PARTS,)),
                dma((chain, CROSS)),
                dma((chain, CROSS)),
                dma((chain // 2,)),
                dma((chain // 2,)),
                dma((members,)),
                dma((members,)),
                dma((members,)),
                dma((members,)),
                dma((members,)),
                dma((members,)),
            ],
            compiler_params=pltpu.CompilerParams(
                collective_id=0, has_side_effects=True, vmem_limit_bytes=63 * 1024 * 1024
            ),
            name="fused_section",
        )(
            section_input,
            conv_taps.T,
            dilation_level[None, :],
            pointwise_matrix.T,
            head_weight,
            pred_error.T,
            tail_mask.T,
            track_scale[None, :],
        )
    )
    return input_grad, taps_grad.T


def local_or_fused(sizes, *args):
    section_input, head_weight, pred_error = args[0], args[4], args[5]
    seq = sizes["seq"]
    fits = (
        sizes["groups"] == 2
        and sizes["track"] == 2
        and seq == 8
        and head_weight.shape[0] % (2 * PARTS * 16) == 0
        and section_input.shape[0] % (seq * 16) == 0
        and section_input.shape[1] % 128 == 0
        and pred_error.shape[1] % 16 == 0
        and pred_error.shape[1] >= 128 * ADJ_PARTS
        and args[3].shape[1] % 32 == 0
        and section_input.shape[0] % 256 == 0
        and section_input.shape[0] // seq <= 128
        and head_weight.shape[0] % (section_input.shape[0] // seq) == 0
    )
    if fits:
        return fused(seq // CROSS, *args)
    return local(*args)


def solution(mesh):
    in_specs = (
        P("track", ("groups", "seq")),
        P(("track", "seq"), None),
        P(("track", "seq")),
        P("track", "seq"),
        P("seq", "track"),
        P(("groups", "seq"), "track"),
        P(("groups", "seq"), "track"),
        P("track"),
    )
    sizes = dict(mesh.shape)
    body = functools.partial(local_or_fused, sizes)
    out_specs = (P("track", ("groups", "seq")), P(("groups", "track", "seq"), None))
    return jax.shard_map(body, mesh=mesh, in_specs=in_specs, out_specs=out_specs, check_vma=False)
```

```python
import functools
import math

import jax
import jax.numpy as jnp
from jax import lax
from jax.experimental import pallas as pl
from jax.experimental.pallas import tpu as pltpu
from jax.sharding import PartitionSpec as P

DILATION_COUNT = 5
BASE_DILATION = 32


root_half = 0.7071067811865476
norm_const = 0.3989422804014327


def gelu_slope(value):
    return 0.5 * (1.0 + jax.scipy.special.erf(value * root_half)) + value * norm_const * jnp.exp(
        -0.5 * value * value
    )


def taps_at(buffer, onehot, margin, sign):
    width_own = buffer.shape[1] - 2 * margin
    result = jnp.zeros((buffer.shape[0], width_own), jnp.float32)
    for level_index in range(onehot.shape[1]):
        receptive_span = BASE_DILATION * 2**level_index
        begin = margin + sign * receptive_span
        result = (
            result + onehot[:, level_index : level_index + 1] * buffer[:, begin : begin + width_own]
        )
    return result


def spread(values, onehot, margin, sign):
    result = jnp.zeros((values.shape[0], values.shape[1] + 2 * margin), jnp.float32)
    for level_index in range(onehot.shape[1]):
        receptive_span = BASE_DILATION * 2**level_index
        placed = onehot[:, level_index : level_index + 1] * values
        result = result + jnp.pad(
            placed, ((0, 0), (margin + sign * receptive_span, margin - sign * receptive_span))
        )
    return result


def channel_grads(buffer, hidden_grad, taps, onehot, margin):
    width_own = buffer.shape[1] - 2 * margin
    minus_side = taps_at(buffer, onehot, margin, -1)
    center = buffer[:, margin : margin + width_own]
    plus_side = taps_at(buffer, onehot, margin, 1)
    pre_act = taps[:, 0:1] * minus_side + taps[:, 1:2] * center + taps[:, 2:3] * plus_side
    pre_grad = hidden_grad.astype(jnp.float32) * gelu_slope(pre_act)
    taps_part = jnp.stack(
        [
            jnp.sum(pre_grad * minus_side, axis=1),
            jnp.sum(pre_grad * center, axis=1),
            jnp.sum(pre_grad * plus_side, axis=1),
        ],
        axis=1,
    )
    contrib = spread(taps[:, 0:1] * pre_grad, onehot, margin, -1) + spread(
        taps[:, 2:3] * pre_grad, onehot, margin, 1
    )
    contrib = contrib + jnp.pad(taps[:, 1:2] * pre_grad, ((0, 0), (margin, margin)))
    return (contrib, taps_part)


def local(
    section_input,
    conv_taps,
    dilation_level,
    pointwise_matrix,
    head_weight,
    pred_error,
    tail_mask,
    track_scale,
):
    own_channels = section_input.shape[0]
    own_rows = section_input.shape[1]
    adjoint = (
        tail_mask.astype(jnp.float32) * track_scale[None, :] * pred_error.astype(jnp.float32)
    ).astype(jnp.bfloat16)
    full_grad = lax.dot_general(
        lax.all_gather(head_weight, "seq", axis=0, tiled=True),
        adjoint,
        (((1,), (1,)), ((), ())),
        preferred_element_type=jnp.float32,
    )
    total = lax.psum(full_grad, "track")
    out_grad_b = total.astype(jnp.bfloat16)
    out_grad = lax.dynamic_slice_in_dim(
        total, lax.axis_index("track") * own_channels, own_channels, 0
    )
    hidden_grad = jnp.dot(
        lax.all_gather(pointwise_matrix, "seq", axis=1, tiled=True),
        out_grad_b,
        preferred_element_type=jnp.float32,
    ).astype(jnp.bfloat16)
    largest_span = BASE_DILATION * 2 ** (DILATION_COUNT - 1)
    scale = 1.0 / math.sqrt(own_rows * lax.axis_size("seq"))
    onehot = (
        dilation_level[:, None] == jnp.arange(DILATION_COUNT, dtype=jnp.int32)[None, :]
    ).astype(jnp.float32)
    owned_input, owned_grad = (
        lax.all_to_all(section_input, "seq", split_axis=0, concat_axis=1, tiled=True),
        lax.all_to_all(hidden_grad, "seq", split_axis=0, concat_axis=1, tiled=True),
    )
    padded = jnp.pad(owned_input.astype(jnp.float32), ((0, 0), (largest_span, largest_span)))
    contrib, taps_part = channel_grads(padded, owned_grad, conv_taps, onehot, largest_span)
    window = contrib[:, largest_span : largest_span + owned_input.shape[1]]
    conv_part = lax.all_to_all(window, "seq", split_axis=1, concat_axis=0, tiled=True)
    taps_grad = taps_part * scale
    input_grad = (out_grad + conv_part).astype(jnp.bfloat16)
    return (input_grad, taps_grad)


MESH = pl.DeviceIdType.MESH
CROSS = 2
PARTS = 6
ADJ_PARTS = 4
BACK_PARTS = 3


def fused_kernel(
    chain,
    sec,
    taps,
    level,
    pw,
    hw,
    err,
    mask,
    scale,
    out,
    tg,
    wb,
    ab,
    ev,
    mv,
    pb,
    gp,
    gr,
    ob,
    ox,
    hs,
    hr,
    xr,
    xp,
    hx,
    hq,
    cb,
    rb,
    cols,
    sums,
    ld_sem,
    w_send,
    w_recv,
    wy_send,
    wy_recv,
    p_send,
    p_recv,
    py_send,
    py_recv,
    a_send,
    a_recv,
    g_send,
    g_recv,
    o_send,
    o_recv,
    x_send,
    x_recv,
    c_send,
    c_recv,
    h_send,
    h_recv,
    r_send,
    r_recv,
):
    g = lax.axis_index("groups")
    s = lax.axis_index("seq")
    t = lax.axis_index("track")
    members = chain * CROSS
    z = s // CROSS
    x = s % CROSS
    head_rows = hw.shape[0]
    half = head_rows // 2
    piece = half // PARTS
    tracks, own_rows = err.shape
    own = sec.shape[0]
    owned = own // members
    phalf = pw.shape[0] // 2
    step = tracks // ADJ_PARTS // 128 * 128
    cuts = [c * step for c in range(ADJ_PARTS)] + [tracks]
    pair_rows = CROSS * own_rows
    length = members * own_rows
    span = xp.shape[1] - length

    sibling = (g, s, 1 - t)
    twin = (1 - g, s, t)
    across = (g, z * CROSS + 1 - x, t)

    def peer(k):
        return lax.rem(s + k, members)

    barrier = pltpu.get_barrier_semaphore()

    def greet(k, carry):
        pl.semaphore_signal(barrier, inc=1, device_id=(g, peer(k), t), device_id_type=MESH)
        return carry

    lax.fori_loop(1, members, greet, 0)
    pl.semaphore_signal(barrier, inc=1, device_id=sibling, device_id_type=MESH)
    pl.semaphore_signal(barrier, inc=1, device_id=twin, device_id_type=MESH)

    own_w = pltpu.make_async_copy(
        hw, wb.at[pl.ds(pl.multiple_of(z * head_rows, 16), head_rows), :], ld_sem.at[0]
    )
    own_p = pltpu.make_async_copy(pw, pb.at[z], ld_sem.at[1])
    own_x = pltpu.make_async_copy(sec.at[pl.ds(pl.multiple_of(s * owned, 16), owned), :], xr.at[s], ld_sem.at[2])
    loads = []
    for c in range(ADJ_PARTS):
        rows = pl.ds(cuts[c], cuts[c + 1] - cuts[c])
        loads.append(
            (
                pltpu.make_async_copy(err.at[rows, :], ev.at[rows, :], ld_sem.at[3 + 2 * c]),
                pltpu.make_async_copy(mask.at[rows, :], mv.at[rows, :], ld_sem.at[4 + 2 * c]),
            )
        )
    for first, second in loads:
        first.start()
        second.start()
    own_w.start()
    own_p.start()
    own_x.start()
    pl.semaphore_wait(barrier, members - 1 + 2)

    def w_rows(shard, c, which):
        return pl.ds(pl.multiple_of(shard * head_rows + which * half + c * piece, 16), piece)

    def w_hop(shard, c, src, toward, direction):
        slot = shard * PARTS + c
        return pltpu.make_async_remote_copy(
            src_ref=src,
            dst_ref=wb.at[w_rows(shard, c, g), :],
            send_sem=w_send.at[direction, slot],
            recv_sem=w_recv.at[slot],
            device_id=(g, toward * CROSS + x, t),
            device_id_type=MESH,
        )

    def w_swap(shard, c, which):
        slot = shard * PARTS + c
        block = wb.at[w_rows(shard, c, which), :]
        return pltpu.make_async_remote_copy(
            src_ref=block,
            dst_ref=block,
            send_sem=wy_send.at[slot],
            recv_sem=wy_recv.at[slot],
            device_id=twin,
            device_id_type=MESH,
        )

    def p_hop(shard, src, toward, direction):
        return pltpu.make_async_remote_copy(
            src_ref=src,
            dst_ref=pb.at[shard, pl.ds(pl.multiple_of(g * phalf, 16), phalf), :],
            send_sem=p_send.at[direction, shard],
            recv_sem=p_recv.at[shard],
            device_id=(g, toward * CROSS + x, t),
            device_id_type=MESH,
        )

    def p_swap(shard, which):
        block = pb.at[shard, pl.ds(pl.multiple_of(which * phalf, 16), phalf), :]
        return pltpu.make_async_remote_copy(
            src_ref=block,
            dst_ref=block,
            send_sem=py_send.at[shard],
            recv_sem=py_recv.at[shard],
            device_id=twin,
            device_id_type=MESH,
        )

    has_up = z < chain - 1
    has_down = z > 0

    def own_piece(c):
        return hw.at[pl.ds(pl.multiple_of(g * half + c * piece, 16), piece), :]

    own_phalf = pw.at[pl.ds(pl.multiple_of(g * phalf, 16), phalf), :]

    @pl.when(has_up)
    def _():
        for c in range(PARTS):
            w_hop(z, c, own_piece(c), z + 1, 0).start()

    @pl.when(has_down)
    def _():
        for c in range(PARTS):
            w_hop(z, c, own_piece(c), z - 1, 1).start()

    def a_copy(c):
        rows = pl.ds(cuts[c], cuts[c + 1] - cuts[c])
        block = ab.at[x, rows, :]
        return pltpu.make_async_remote_copy(
            src_ref=block,
            dst_ref=block,
            send_sem=a_send.at[c],
            recv_sem=a_recv.at[c],
            device_id=across,
            device_id_type=MESH,
        )

    for c in range(ADJ_PARTS):
        loads[c][0].wait()
        loads[c][1].wait()

        def fill(begin, count):
            rows = pl.ds(begin, count)
            line = scale[rows].reshape(1, count)
            if count < 128:
                line = jnp.concatenate([line, jnp.zeros((1, 128 - count), jnp.float32)], axis=1)
            column = jnp.transpose(jnp.broadcast_to(line, (128, 128)))[:count]
            column = jnp.concatenate([column] * (own_rows // 128), axis=1)
            value = mv[rows, :].astype(jnp.float32) * column * ev[rows, :].astype(jnp.float32)
            ab[x, rows, :] = value.astype(jnp.bfloat16)

        def fill_step(i, carry):
            fill(pl.multiple_of(cuts[c] + i * 128, 128), 128)
            return carry

        whole, rest = divmod(cuts[c + 1] - cuts[c], 128)
        lax.fori_loop(0, whole, fill_step, 0)
        if rest:
            fill(cuts[c] + whole * 128, rest)
        a_copy(c).start()

    @pl.when(has_up)
    def _():
        p_hop(z, own_phalf, z + 1, 0).start()

    @pl.when(has_down)
    def _():
        p_hop(z, own_phalf, z - 1, 1).start()

    def x_copy(to, frm):
        return pltpu.make_async_remote_copy(
            src_ref=sec.at[pl.ds(pl.multiple_of(to * owned, 16), owned), :],
            dst_ref=xr.at[frm],
            send_sem=x_send.at[to],
            recv_sem=x_recv.at[frm],
            device_id=(g, to, t),
            device_id_type=MESH,
        )

    def x_start(k, carry):
        x_copy(peer(k), s).start()
        return carry


    below = z
    above = chain - 1 - z
    near = jnp.minimum(below, above)

    def order(j):
        step = (j + 1) // 2
        alternate = jnp.where(j % 2 == 1, z - step, z + step)
        one_sided = jnp.where(above > below, z + (j - near), z - (j - near))
        return jnp.where(j <= 2 * near, alternate, one_sided)

    def g_copy(shard, xs):
        rows = pl.ds(pl.multiple_of(shard * head_rows, 16), head_rows)
        return pltpu.make_async_remote_copy(
            src_ref=gp.at[xs, rows, :],
            dst_ref=gr.at[xs, rows, :],
            send_sem=g_send.at[shard, xs],
            recv_sem=g_recv.at[shard, xs],
            device_id=sibling,
            device_id_type=MESH,
        )

    def head_dot(shard, xs):
        rows = pl.ds(pl.multiple_of(shard * head_rows, 16), head_rows)
        gp[xs, rows, :] = lax.dot_general(
            wb[rows, :],
            ab[xs],
            (((1,), (0,)), ((), ())),
            preferred_element_type=jnp.float32,
        )
        g_copy(shard, xs).start()

    def w_relay(e, carry):
        paired = (near >= 1) & (e < 2 * PARTS)
        j = jnp.where(paired, 1 + e % 2, e // PARTS + 1)
        c = jnp.where(paired, e // 2, e % PARTS)
        shard = order(j)
        block = wb.at[w_rows(shard, c, g), :]
        w_hop(shard, c, block, z, 0).wait_recv()

        @pl.when((shard < z) & has_up)
        def _():
            w_hop(shard, c, block, z + 1, 0).start()

        @pl.when((shard > z) & has_down)
        def _():
            w_hop(shard, c, block, z - 1, 1).start()

        w_swap(shard, c, g).start()
        return carry

    def wait_swaps(shard):
        def one(c, carry):
            w_swap(shard, c, 1 - g).wait_recv()
            return carry

        lax.fori_loop(0, PARTS, one, 0)

    own_w.wait()
    head_dot(z, x)
    steps = chain - 1
    lax.fori_loop(0, (steps - 1) * PARTS, w_relay, 0)

    def early(j, carry):
        shard = order(j)
        wait_swaps(shard)
        head_dot(shard, x)
        return carry

    lax.fori_loop(1, steps - 1, early, 0)
    lax.fori_loop((steps - 1) * PARTS, steps * PARTS, w_relay, 0)
    lax.fori_loop(jnp.maximum(steps - 1, 1), steps, early, 0)

    for c in range(ADJ_PARTS):
        block = ab.at[1 - x, pl.ds(cuts[c], cuts[c + 1] - cuts[c]), :]
        pltpu.make_async_remote_copy(
            src_ref=block,
            dst_ref=block,
            send_sem=a_send.at[c],
            recv_sem=a_recv.at[c],
            device_id=across,
            device_id_type=MESH,
        ).wait_recv()

    def late(j, carry):
        head_dot(jnp.where(j == 0, z, order(jnp.maximum(j, 1))), 1 - x)
        return carry

    lax.fori_loop(0, steps, late, 0)

    def p_relay(j, carry):
        shard = order(j)
        block = pb.at[shard, pl.ds(pl.multiple_of(g * phalf, 16), phalf), :]
        p_hop(shard, block, z, 0).wait_recv()

        @pl.when((shard < z) & has_up)
        def _():
            p_hop(shard, block, z + 1, 0).start()

        @pl.when((shard > z) & has_down)
        def _():
            p_hop(shard, block, z - 1, 1).start()

        p_swap(shard, g).start()
        return carry

    lax.fori_loop(1, steps + 1, p_relay, 0)
    lax.fori_loop(1, members, x_start, 0)
    last = order(steps)
    wait_swaps(last)
    head_dot(last, x)
    head_dot(last, 1 - x)

    def core_sum(j, carry):
        shard = jnp.where(j == 0, z, order(jnp.maximum(j, 1)))
        rows = pl.ds(pl.multiple_of(shard * head_rows, 16), head_rows)
        for xs in range(CROSS):
            g_copy(shard, xs).wait_recv()
            ob[rows, xs * own_rows : (xs + 1) * own_rows] = (gp[xs, rows, :] + gr[xs, rows, :]).astype(
                jnp.bfloat16
            )
        return carry

    lax.fori_loop(0, chain, core_sum, 0)

    blocks_kept = chain // 2

    def o_copy(q):
        return pltpu.make_async_remote_copy(
            src_ref=ob.at[
                pl.ds(pl.multiple_of((t * blocks_kept + q) * head_rows, 16), head_rows),
                pl.ds(pl.multiple_of((1 - x) * own_rows, 128), own_rows),
            ],
            dst_ref=ox.at[q],
            send_sem=o_send.at[q],
            recv_sem=o_recv.at[q],
            device_id=across,
            device_id_type=MESH,
        )

    for q in range(blocks_kept):
        o_copy(q).start()

    own_p.wait()

    def p_wait(j, carry):
        p_swap(order(j), 1 - g).wait_recv()
        return carry

    lax.fori_loop(1, steps + 1, p_wait, 0)

    def h_rows(to):
        return pl.ds(pl.multiple_of(to * owned, 16), owned)

    def c_copy(level_z):
        return pltpu.make_async_remote_copy(
            src_ref=hs.at[h_rows(level_z * CROSS + 1 - x), :],
            dst_ref=hx.at[level_z],
            send_sem=c_send.at[level_z],
            recv_sem=c_recv.at[level_z],
            device_id=across,
            device_id_type=MESH,
        )

    def h_copy(to, frm):
        return pltpu.make_async_remote_copy(
            src_ref=hq.at[to],
            dst_ref=hr.at[frm],
            send_sem=h_send.at[to],
            recv_sem=h_recv.at[frm],
            device_id=(g, to * CROSS + x, t),
            device_id_type=MESH,
        )

    group = members // 2
    wide_rows = group * owned

    def h_step(k, carry):
        n = (s // group + 1 + k) % 2
        lanes = pl.ds(pl.multiple_of(n * wide_rows, 128), wide_rows)
        total = jnp.zeros((wide_rows, pair_rows), jnp.float32)
        for shard in range(chain):
            total = total + lax.dot_general(
                pb[shard, :, lanes],
                ob[shard * head_rows : (shard + 1) * head_rows, :],
                (((0,), (0,)), ((), ())),
                preferred_element_type=jnp.float32,
            )
        hs[lanes, :] = total.astype(jnp.bfloat16)
        for u in range(group // CROSS):
            c_copy(n * (group // CROSS) + u).start()
        return carry

    lax.fori_loop(0, 2, h_step, 0)

    def h_sum(to):
        c_copy(to).wait_recv()
        mine = hs[h_rows(to * CROSS + x), :].astype(jnp.float32)
        return (mine + hx[to].astype(jnp.float32)).astype(jnp.bfloat16)

    def h_pass(k, carry):
        to = order(steps - k)
        hq[to] = h_sum(to)
        h_copy(to, z).start()
        return carry

    lax.fori_loop(0, steps, h_pass, 0)
    hr[z] = h_sum(z)

    own_x.wait()

    def x_wait(k, carry):
        x_copy(s, peer(k)).wait_recv()
        return carry

    lax.fori_loop(1, members, x_wait, 0)
    for m in range(members):
        xp[:, m * own_rows : (m + 1) * own_rows] = xr[m].astype(jnp.float32)
    xp[:, length:] = jnp.zeros((owned, span), jnp.float32)

    columns = cols.at[1]
    cols[0] = jnp.zeros((128, 128), jnp.float32)
    cols[0, 0:3, 0:owned] = taps[...]
    cols[0, 3:4, 0:owned] = level[...].astype(jnp.float32)
    cols[1] = jnp.transpose(cols[0])
    sums[...] = jnp.zeros((128, 128), jnp.float32)

    def h_wait(j, carry):
        h_copy(z, order(j)).wait_recv()
        return carry

    lax.fori_loop(1, steps + 1, h_wait, 0)

    padded = length + span
    norm = 1.0 / math.sqrt(length)

    def conv_rows(i, carry):
        rows = pl.ds(pl.multiple_of(i * 16, 16), 16)
        lev = columns[rows, 3:4]
        tap = columns[rows, 0:3]

        def pick(value, sign):
            result = None
            for k in range(DILATION_COUNT):
                reach = BASE_DILATION * 2**k
                moved = pltpu.roll(value, reach if sign < 0 else padded - reach, 1)[:, :length]
                result = moved if result is None else jnp.where(lev == float(k), moved, result)
            return result

        wide = xp[rows, :]
        minus = pick(wide, -1)
        plus = pick(wide, 1)
        center = wide[:, :length]
        pre_act = tap[:, 0:1] * minus + tap[:, 1:2] * center + tap[:, 2:3] * plus
        hidden = jnp.concatenate([hr[m, rows, :] for m in range(chain)], axis=1)
        pre_grad = hidden.astype(jnp.float32) * gelu_slope(pre_act)
        sums[rows, 0:1] = jnp.sum(pre_grad * minus, axis=1, keepdims=True) * norm
        sums[rows, 1:2] = jnp.sum(pre_grad * center, axis=1, keepdims=True) * norm
        sums[rows, 2:3] = jnp.sum(pre_grad * plus, axis=1, keepdims=True) * norm
        spread_wide = jnp.concatenate([pre_grad, jnp.zeros((16, span), jnp.float32)], axis=1)
        part = (
            tap[:, 0:1] * pick(spread_wide, 1)
            + tap[:, 1:2] * pre_grad
            + tap[:, 2:3] * pick(spread_wide, -1)
        ).astype(jnp.bfloat16)
        for m in range(members):
            cb[m, rows, :] = part[:, m * own_rows : (m + 1) * own_rows]
        return carry

    back = owned // BACK_PARTS

    def r_copy(to, frm, c):
        rows = pl.ds(pl.multiple_of(c * back, 16), back)
        return pltpu.make_async_remote_copy(
            src_ref=cb.at[to, rows, :],
            dst_ref=rb.at[frm, rows, :],
            send_sem=r_send.at[to, c],
            recv_sem=r_recv.at[frm, c],
            device_id=(g, to, t),
            device_id_type=MESH,
        )

    def conv_part(c, carry):
        lax.fori_loop(c * (back // 16), (c + 1) * (back // 16), conv_rows, 0)

        def r_start(k, inner):
            r_copy(peer(k), s, c).start()
            return inner

        lax.fori_loop(1, members, r_start, 0)
        return carry

    lax.fori_loop(0, BACK_PARTS, conv_part, 0)
    rb[s] = cb[s]
    for q in range(blocks_kept):
        o_copy(q).wait_recv()

    def r_wait(k, carry):
        for c in range(BACK_PARTS):
            r_copy(s, peer(k), c).wait_recv()
        return carry

    lax.fori_loop(1, members, r_wait, 0)

    per = head_rows // owned
    for q in range(blocks_kept):
        for u in range(per):
            mine = (CROSS * q + x) * per + u
            src = pl.ds(pl.multiple_of((t * blocks_kept + q) * head_rows + u * owned, 16), owned)
            here = jnp.where(
                x == 0, ob[src, 0:own_rows].astype(jnp.float32), ob[src, own_rows:].astype(jnp.float32)
            )
            out[pl.ds(pl.multiple_of(mine * owned, 16), owned), :] = (
                here + rb[mine].astype(jnp.float32)
            ).astype(jnp.bfloat16)
            other = (CROSS * q + 1 - x) * per + u
            there = ox[q, u * owned : (u + 1) * owned, :].astype(jnp.float32)
            out[pl.ds(pl.multiple_of(other * owned, 16), owned), :] = (
                there + rb[other].astype(jnp.float32)
            ).astype(jnp.bfloat16)

    tg[...] = jnp.transpose(sums[...])[0:3, 0:owned]

    def w_done(shard, carry):
        def one(c, inner):
            block = wb.at[w_rows(shard, c, g), :]

            @pl.when((shard <= z) & has_up)
            def _():
                w_hop(shard, c, block, z, 0).wait_send()

            @pl.when((shard >= z) & has_down)
            def _():
                w_hop(shard, c, block, z, 1).wait_send()

            @pl.when(shard != z)
            def _():
                w_swap(shard, c, g).wait_send()

            return inner

        lax.fori_loop(0, PARTS, one, 0)
        pblock = pb.at[shard, pl.ds(pl.multiple_of(g * phalf, 16), phalf), :]

        @pl.when((shard <= z) & has_up)
        def _():
            p_hop(shard, pblock, z, 0).wait_send()

        @pl.when((shard >= z) & has_down)
        def _():
            p_hop(shard, pblock, z, 1).wait_send()

        @pl.when(shard != z)
        def _():
            p_swap(shard, g).wait_send()

        for xs in range(CROSS):
            g_copy(shard, xs).wait_send()
        c_copy(shard).wait_send()

        @pl.when(shard != z)
        def _():
            h_copy(shard, z).wait_send()

        return carry

    lax.fori_loop(0, chain, w_done, 0)

    for c in range(ADJ_PARTS):
        a_copy(c).wait_send()
    for q in range(blocks_kept):
        o_copy(q).wait_send()

    def done(k, carry):
        x_copy(peer(k), s).wait_send()
        for c in range(BACK_PARTS):
            r_copy(peer(k), s, c).wait_send()
        return carry

    lax.fori_loop(1, members, done, 0)


def fused(
    chain,
    section_input,
    conv_taps,
    dilation_level,
    pointwise_matrix,
    head_weight,
    pred_error,
    tail_mask,
    track_scale,
):
    own, own_rows = section_input.shape
    members = chain * CROSS
    owned = own // members
    head_rows, tracks = head_weight.shape
    pair_rows = CROSS * own_rows
    length = members * own_rows
    span = BASE_DILATION * 2 ** (DILATION_COUNT - 1)
    cols = pointwise_matrix.shape[1]
    bf16, f32 = jnp.bfloat16, jnp.float32
    dma = pltpu.SemaphoreType.DMA
    anywhere = pl.BlockSpec(memory_space=pltpu.HBM)
    vmem = pl.BlockSpec(memory_space=pltpu.VMEM)
    input_grad, taps_grad = (
        pl.pallas_call(
            functools.partial(fused_kernel, chain),
            out_shape=(
                jax.ShapeDtypeStruct((own, own_rows), bf16),
                jax.ShapeDtypeStruct((3, owned), f32),
            ),
            in_specs=[anywhere, vmem, vmem, anywhere, anywhere, anywhere, anywhere, vmem],
            out_specs=(vmem, vmem),
            scratch_shapes=[
                pltpu.VMEM((chain * head_rows, tracks), bf16),
                pltpu.VMEM((CROSS, tracks, own_rows), bf16),
                pltpu.VMEM((tracks, own_rows), bf16),
                pltpu.VMEM((tracks, own_rows), jnp.int32),
                pltpu.VMEM((chain, cols, own), bf16),
                pltpu.VMEM((CROSS, chain * head_rows, own_rows), f32),
                pltpu.VMEM((CROSS, chain * head_rows, own_rows), f32),
                pltpu.VMEM((chain * head_rows, pair_rows), bf16),
                pltpu.VMEM((chain // 2, head_rows, own_rows), bf16),
                pltpu.VMEM((own, pair_rows), bf16),
                pltpu.VMEM((chain, owned, pair_rows), bf16),
                pltpu.VMEM((members, owned, own_rows), bf16),
                pltpu.VMEM((owned, length + span), f32),
                pltpu.VMEM((chain, owned, pair_rows), bf16),
                pltpu.VMEM((chain, owned, pair_rows), bf16),
                pltpu.VMEM((members, owned, own_rows), bf16),
                pltpu.VMEM((members, owned, own_rows), bf16),
                pltpu.VMEM((2, 128, 128), f32),
                pltpu.VMEM((128, 128), f32),
                dma((3 + 2 * ADJ_PARTS,)),
                dma((2, chain * PARTS)),
                dma((chain * PARTS,)),
                dma((chain * PARTS,)),
                dma((chain * PARTS,)),
                dma((2, chain)),
                dma((chain,)),
                dma((chain,)),
                dma((chain,)),
                dma((ADJ_PARTS,)),
                dma((ADJ_PARTS,)),
                dma((chain, CROSS)),
                dma((chain, CROSS)),
                dma((chain // 2,)),
                dma((chain // 2,)),
                dma((members,)),
                dma((members,)),
                dma((chain,)),
                dma((chain,)),
                dma((chain,)),
                dma((chain,)),
                dma((members, BACK_PARTS)),
                dma((members, BACK_PARTS)),
            ],
            compiler_params=pltpu.CompilerParams(
                collective_id=0, has_side_effects=True, vmem_limit_bytes=63 * 1024 * 1024
            ),
            name="fused_section",
        )(
            section_input,
            conv_taps.T,
            dilation_level[None, :],
            pointwise_matrix.T,
            head_weight,
            pred_error.T,
            tail_mask.T,
            track_scale,
        )
    )
    return input_grad, taps_grad.T


def local_or_fused(sizes, *args):
    section_input, head_weight, pred_error = args[0], args[4], args[5]
    seq = sizes["seq"]
    fits = (
        sizes["groups"] == 2
        and sizes["track"] == 2
        and seq == 8
        and head_weight.shape[0] % (2 * PARTS * 16) == 0
        and section_input.shape[0] % (seq * 16) == 0
        and section_input.shape[1] % 128 == 0
        and pred_error.shape[1] % 16 == 0
        and pred_error.shape[1] >= 128 * ADJ_PARTS
        and args[3].shape[1] % 32 == 0
        and section_input.shape[0] % 256 == 0
        and section_input.shape[0] // seq <= 128
        and section_input.shape[0] // seq % (BACK_PARTS * 16) == 0
        and head_weight.shape[0] % (section_input.shape[0] // seq) == 0
    )
    if fits:
        return fused(seq // CROSS, *args)
    return local(*args)


def solution(mesh):
    in_specs = (
        P("track", ("groups", "seq")),
        P(("track", "seq"), None),
        P(("track", "seq")),
        P("track", "seq"),
        P("seq", "track"),
        P(("groups", "seq"), "track"),
        P(("groups", "seq"), "track"),
        P("track"),
    )
    sizes = dict(mesh.shape)
    body = functools.partial(local_or_fused, sizes)
    out_specs = (P("track", ("groups", "seq")), P(("groups", "track", "seq"), None))
    return jax.shard_map(body, mesh=mesh, in_specs=in_specs, out_specs=out_specs, check_vma=False)
```

```python
import functools
import math

import jax
import jax.numpy as jnp
from jax import lax
from jax.experimental import pallas as pl
from jax.experimental.pallas import tpu as pltpu
from jax.sharding import PartitionSpec as P

DILATION_COUNT = 5
BASE_DILATION = 32


root_half = 0.7071067811865476
norm_const = 0.3989422804014327


def gelu_slope(value):
    return 0.5 * (1.0 + jax.scipy.special.erf(value * root_half)) + value * norm_const * jnp.exp(
        -0.5 * value * value
    )


def taps_at(buffer, onehot, margin, sign):
    width_own = buffer.shape[1] - 2 * margin
    result = jnp.zeros((buffer.shape[0], width_own), jnp.float32)
    for level_index in range(onehot.shape[1]):
        receptive_span = BASE_DILATION * 2**level_index
        begin = margin + sign * receptive_span
        result = (
            result + onehot[:, level_index : level_index + 1] * buffer[:, begin : begin + width_own]
        )
    return result


def spread(values, onehot, margin, sign):
    result = jnp.zeros((values.shape[0], values.shape[1] + 2 * margin), jnp.float32)
    for level_index in range(onehot.shape[1]):
        receptive_span = BASE_DILATION * 2**level_index
        placed = onehot[:, level_index : level_index + 1] * values
        result = result + jnp.pad(
            placed, ((0, 0), (margin + sign * receptive_span, margin - sign * receptive_span))
        )
    return result


def channel_grads(buffer, hidden_grad, taps, onehot, margin):
    width_own = buffer.shape[1] - 2 * margin
    minus_side = taps_at(buffer, onehot, margin, -1)
    center = buffer[:, margin : margin + width_own]
    plus_side = taps_at(buffer, onehot, margin, 1)
    pre_act = taps[:, 0:1] * minus_side + taps[:, 1:2] * center + taps[:, 2:3] * plus_side
    pre_grad = hidden_grad.astype(jnp.float32) * gelu_slope(pre_act)
    taps_part = jnp.stack(
        [
            jnp.sum(pre_grad * minus_side, axis=1),
            jnp.sum(pre_grad * center, axis=1),
            jnp.sum(pre_grad * plus_side, axis=1),
        ],
        axis=1,
    )
    contrib = spread(taps[:, 0:1] * pre_grad, onehot, margin, -1) + spread(
        taps[:, 2:3] * pre_grad, onehot, margin, 1
    )
    contrib = contrib + jnp.pad(taps[:, 1:2] * pre_grad, ((0, 0), (margin, margin)))
    return (contrib, taps_part)


def local(
    section_input,
    conv_taps,
    dilation_level,
    pointwise_matrix,
    head_weight,
    pred_error,
    tail_mask,
    track_scale,
):
    own_channels = section_input.shape[0]
    own_rows = section_input.shape[1]
    adjoint = (
        tail_mask.astype(jnp.float32) * track_scale[None, :] * pred_error.astype(jnp.float32)
    ).astype(jnp.bfloat16)
    full_grad = lax.dot_general(
        lax.all_gather(head_weight, "seq", axis=0, tiled=True),
        adjoint,
        (((1,), (1,)), ((), ())),
        preferred_element_type=jnp.float32,
    )
    total = lax.psum(full_grad, "track")
    out_grad_b = total.astype(jnp.bfloat16)
    out_grad = lax.dynamic_slice_in_dim(
        total, lax.axis_index("track") * own_channels, own_channels, 0
    )
    hidden_grad = jnp.dot(
        lax.all_gather(pointwise_matrix, "seq", axis=1, tiled=True),
        out_grad_b,
        preferred_element_type=jnp.float32,
    ).astype(jnp.bfloat16)
    largest_span = BASE_DILATION * 2 ** (DILATION_COUNT - 1)
    scale = 1.0 / math.sqrt(own_rows * lax.axis_size("seq"))
    onehot = (
        dilation_level[:, None] == jnp.arange(DILATION_COUNT, dtype=jnp.int32)[None, :]
    ).astype(jnp.float32)
    owned_input, owned_grad = (
        lax.all_to_all(section_input, "seq", split_axis=0, concat_axis=1, tiled=True),
        lax.all_to_all(hidden_grad, "seq", split_axis=0, concat_axis=1, tiled=True),
    )
    padded = jnp.pad(owned_input.astype(jnp.float32), ((0, 0), (largest_span, largest_span)))
    contrib, taps_part = channel_grads(padded, owned_grad, conv_taps, onehot, largest_span)
    window = contrib[:, largest_span : largest_span + owned_input.shape[1]]
    conv_part = lax.all_to_all(window, "seq", split_axis=1, concat_axis=0, tiled=True)
    taps_grad = taps_part * scale
    input_grad = (out_grad + conv_part).astype(jnp.bfloat16)
    return (input_grad, taps_grad)


MESH = pl.DeviceIdType.MESH
CROSS = 2
PARTS = 6
ADJ_PARTS = 4
BACK_PARTS = 3
P_PARTS = 3


def fused_kernel(
    chain,
    sec,
    taps,
    level,
    pw,
    hw,
    err,
    mask,
    scale,
    out,
    tg,
    wb,
    ab,
    ev,
    mv,
    pb,
    gp,
    gr,
    ob,
    ox,
    hs,
    hr,
    xr,
    xp,
    hx,
    hq,
    cb,
    rb,
    cols,
    sums,
    ld_sem,
    w_send,
    w_recv,
    wy_send,
    wy_recv,
    p_send,
    p_recv,
    py_send,
    py_recv,
    a_send,
    a_recv,
    g_send,
    g_recv,
    o_send,
    o_recv,
    x_send,
    x_recv,
    c_send,
    c_recv,
    h_send,
    h_recv,
    r_send,
    r_recv,
):
    g = lax.axis_index("groups")
    s = lax.axis_index("seq")
    t = lax.axis_index("track")
    members = chain * CROSS
    z = s // CROSS
    x = s % CROSS
    head_rows = hw.shape[0]
    half = head_rows // 2
    piece = half // PARTS
    tracks, own_rows = err.shape
    own = sec.shape[0]
    owned = own // members
    phalf = pw.shape[0] // 2
    step = tracks // ADJ_PARTS // 128 * 128
    cuts = [c * step for c in range(ADJ_PARTS)] + [tracks]
    pair_rows = CROSS * own_rows
    length = members * own_rows
    span = xp.shape[1] - length

    sibling = (g, s, 1 - t)
    twin = (1 - g, s, t)
    across = (g, z * CROSS + 1 - x, t)

    def peer(k):
        return lax.rem(s + k, members)

    barrier = pltpu.get_barrier_semaphore()

    def greet(k, carry):
        pl.semaphore_signal(barrier, inc=1, device_id=(g, peer(k), t), device_id_type=MESH)
        return carry

    lax.fori_loop(1, members, greet, 0)
    pl.semaphore_signal(barrier, inc=1, device_id=sibling, device_id_type=MESH)
    pl.semaphore_signal(barrier, inc=1, device_id=twin, device_id_type=MESH)

    own_w = pltpu.make_async_copy(
        hw, wb.at[pl.ds(pl.multiple_of(z * head_rows, 16), head_rows), :], ld_sem.at[0]
    )
    own_p = pltpu.make_async_copy(pw, pb.at[z], ld_sem.at[1])
    own_x = pltpu.make_async_copy(sec.at[pl.ds(pl.multiple_of(s * owned, 16), owned), :], xr.at[s], ld_sem.at[2])
    loads = []
    for c in range(ADJ_PARTS):
        rows = pl.ds(cuts[c], cuts[c + 1] - cuts[c])
        loads.append(
            (
                pltpu.make_async_copy(err.at[rows, :], ev.at[rows, :], ld_sem.at[3 + 2 * c]),
                pltpu.make_async_copy(mask.at[rows, :], mv.at[rows, :], ld_sem.at[4 + 2 * c]),
            )
        )
    for first, second in loads:
        first.start()
        second.start()
    own_w.start()
    own_p.start()
    own_x.start()
    pl.semaphore_wait(barrier, members - 1 + 2)

    def w_rows(shard, c, which):
        return pl.ds(pl.multiple_of(shard * head_rows + which * half + c * piece, 16), piece)

    def w_hop(shard, c, src, toward, direction):
        slot = shard * PARTS + c
        return pltpu.make_async_remote_copy(
            src_ref=src,
            dst_ref=wb.at[w_rows(shard, c, g), :],
            send_sem=w_send.at[direction, slot],
            recv_sem=w_recv.at[slot],
            device_id=(g, toward * CROSS + x, t),
            device_id_type=MESH,
        )

    def w_swap(shard, c, which):
        slot = shard * PARTS + c
        block = wb.at[w_rows(shard, c, which), :]
        return pltpu.make_async_remote_copy(
            src_ref=block,
            dst_ref=block,
            send_sem=wy_send.at[slot],
            recv_sem=wy_recv.at[slot],
            device_id=twin,
            device_id_type=MESH,
        )

    p_piece = phalf // P_PARTS

    def p_rows(c, which):
        return pl.ds(pl.multiple_of(which * phalf + c * p_piece, 16), p_piece)

    def p_hop(shard, c, src, toward, direction):
        slot = shard * P_PARTS + c
        return pltpu.make_async_remote_copy(
            src_ref=src,
            dst_ref=pb.at[shard, p_rows(c, g), :],
            send_sem=p_send.at[direction, slot],
            recv_sem=p_recv.at[slot],
            device_id=(g, toward * CROSS + x, t),
            device_id_type=MESH,
        )

    def p_swap(shard, c, which):
        slot = shard * P_PARTS + c
        block = pb.at[shard, p_rows(c, which), :]
        return pltpu.make_async_remote_copy(
            src_ref=block,
            dst_ref=block,
            send_sem=py_send.at[slot],
            recv_sem=py_recv.at[slot],
            device_id=twin,
            device_id_type=MESH,
        )

    has_up = z < chain - 1
    has_down = z > 0

    def own_piece(c):
        return hw.at[pl.ds(pl.multiple_of(g * half + c * piece, 16), piece), :]


    @pl.when(has_up)
    def _():
        for c in range(PARTS):
            w_hop(z, c, own_piece(c), z + 1, 0).start()

    @pl.when(has_down)
    def _():
        for c in range(PARTS):
            w_hop(z, c, own_piece(c), z - 1, 1).start()

    def a_copy(c):
        rows = pl.ds(cuts[c], cuts[c + 1] - cuts[c])
        block = ab.at[x, rows, :]
        return pltpu.make_async_remote_copy(
            src_ref=block,
            dst_ref=block,
            send_sem=a_send.at[c],
            recv_sem=a_recv.at[c],
            device_id=across,
            device_id_type=MESH,
        )

    for c in range(ADJ_PARTS):
        loads[c][0].wait()
        loads[c][1].wait()

        def fill(begin, count):
            rows = pl.ds(begin, count)
            line = scale[rows].reshape(1, count)
            if count < 128:
                line = jnp.concatenate([line, jnp.zeros((1, 128 - count), jnp.float32)], axis=1)
            column = jnp.transpose(jnp.broadcast_to(line, (128, 128)))[:count]
            column = jnp.concatenate([column] * (own_rows // 128), axis=1)
            value = mv[rows, :].astype(jnp.float32) * column * ev[rows, :].astype(jnp.float32)
            ab[x, rows, :] = value.astype(jnp.bfloat16)

        def fill_step(i, carry):
            fill(pl.multiple_of(cuts[c] + i * 128, 128), 128)
            return carry

        whole, rest = divmod(cuts[c + 1] - cuts[c], 128)
        lax.fori_loop(0, whole, fill_step, 0)
        if rest:
            fill(cuts[c] + whole * 128, rest)
        a_copy(c).start()

    @pl.when(has_up)
    def _():
        for c in range(P_PARTS):
            p_hop(z, c, pw.at[p_rows(c, g), :], z + 1, 0).start()

    @pl.when(has_down)
    def _():
        for c in range(P_PARTS):
            p_hop(z, c, pw.at[p_rows(c, g), :], z - 1, 1).start()

    def x_copy(to, frm):
        return pltpu.make_async_remote_copy(
            src_ref=sec.at[pl.ds(pl.multiple_of(to * owned, 16), owned), :],
            dst_ref=xr.at[frm],
            send_sem=x_send.at[to],
            recv_sem=x_recv.at[frm],
            device_id=(g, to, t),
            device_id_type=MESH,
        )

    def x_start(k, carry):
        x_copy(peer(k), s).start()
        return carry


    below = z
    above = chain - 1 - z
    near = jnp.minimum(below, above)

    def order(j):
        step = (j + 1) // 2
        alternate = jnp.where(j % 2 == 1, z - step, z + step)
        one_sided = jnp.where(above > below, z + (j - near), z - (j - near))
        return jnp.where(j <= 2 * near, alternate, one_sided)

    def g_copy(shard, xs):
        rows = pl.ds(pl.multiple_of(shard * head_rows, 16), head_rows)
        return pltpu.make_async_remote_copy(
            src_ref=gp.at[xs, rows, :],
            dst_ref=gr.at[xs, rows, :],
            send_sem=g_send.at[shard, xs],
            recv_sem=g_recv.at[shard, xs],
            device_id=sibling,
            device_id_type=MESH,
        )

    def head_dot(shard, xs):
        rows = pl.ds(pl.multiple_of(shard * head_rows, 16), head_rows)
        gp[xs, rows, :] = lax.dot_general(
            wb[rows, :],
            ab[xs],
            (((1,), (0,)), ((), ())),
            preferred_element_type=jnp.float32,
        )
        g_copy(shard, xs).start()

    def w_relay(e, carry):
        paired = (near >= 1) & (e < 2 * PARTS)
        j = jnp.where(paired, 1 + e % 2, e // PARTS + 1)
        c = jnp.where(paired, e // 2, e % PARTS)
        shard = order(j)
        block = wb.at[w_rows(shard, c, g), :]
        w_hop(shard, c, block, z, 0).wait_recv()

        @pl.when((shard < z) & has_up)
        def _():
            w_hop(shard, c, block, z + 1, 0).start()

        @pl.when((shard > z) & has_down)
        def _():
            w_hop(shard, c, block, z - 1, 1).start()

        w_swap(shard, c, g).start()
        return carry

    def wait_swaps(shard):
        def one(c, carry):
            w_swap(shard, c, 1 - g).wait_recv()
            return carry

        lax.fori_loop(0, PARTS, one, 0)

    own_w.wait()
    head_dot(z, x)
    steps = chain - 1
    lax.fori_loop(0, (steps - 1) * PARTS, w_relay, 0)

    def early(j, carry):
        shard = order(j)
        wait_swaps(shard)
        head_dot(shard, x)
        return carry

    lax.fori_loop(1, steps - 1, early, 0)
    lax.fori_loop((steps - 1) * PARTS, steps * PARTS, w_relay, 0)
    lax.fori_loop(jnp.maximum(steps - 1, 1), steps, early, 0)

    for c in range(ADJ_PARTS):
        block = ab.at[1 - x, pl.ds(cuts[c], cuts[c + 1] - cuts[c]), :]
        pltpu.make_async_remote_copy(
            src_ref=block,
            dst_ref=block,
            send_sem=a_send.at[c],
            recv_sem=a_recv.at[c],
            device_id=across,
            device_id_type=MESH,
        ).wait_recv()

    def late(j, carry):
        head_dot(jnp.where(j == 0, z, order(jnp.maximum(j, 1))), 1 - x)
        return carry

    lax.fori_loop(0, steps, late, 0)

    def p_relay(e, carry):
        shard = order(e // P_PARTS + 1)
        c = e % P_PARTS
        block = pb.at[shard, p_rows(c, g), :]
        p_hop(shard, c, block, z, 0).wait_recv()

        @pl.when((shard < z) & has_up)
        def _():
            p_hop(shard, c, block, z + 1, 0).start()

        @pl.when((shard > z) & has_down)
        def _():
            p_hop(shard, c, block, z - 1, 1).start()

        p_swap(shard, c, g).start()
        return carry

    lax.fori_loop(0, (steps - 1) * P_PARTS, p_relay, 0)
    last = order(steps)
    wait_swaps(last)
    head_dot(last, x)
    head_dot(last, 1 - x)
    lax.fori_loop(1, members, x_start, 0)
    lax.fori_loop((steps - 1) * P_PARTS, steps * P_PARTS, p_relay, 0)

    def core_sum(j, carry):
        shard = jnp.where(j == 0, z, order(jnp.maximum(j, 1)))
        rows = pl.ds(pl.multiple_of(shard * head_rows, 16), head_rows)
        for xs in range(CROSS):
            g_copy(shard, xs).wait_recv()
            ob[rows, xs * own_rows : (xs + 1) * own_rows] = (gp[xs, rows, :] + gr[xs, rows, :]).astype(
                jnp.bfloat16
            )
        return carry

    lax.fori_loop(0, chain, core_sum, 0)

    blocks_kept = chain // 2

    def o_copy(q):
        return pltpu.make_async_remote_copy(
            src_ref=ob.at[
                pl.ds(pl.multiple_of((t * blocks_kept + q) * head_rows, 16), head_rows),
                pl.ds(pl.multiple_of((1 - x) * own_rows, 128), own_rows),
            ],
            dst_ref=ox.at[q],
            send_sem=o_send.at[q],
            recv_sem=o_recv.at[q],
            device_id=across,
            device_id_type=MESH,
        )

    for q in range(blocks_kept):
        o_copy(q).start()

    own_p.wait()

    def p_wait(j, carry):
        for c in range(P_PARTS):
            p_swap(order(j), c, 1 - g).wait_recv()
        return carry

    lax.fori_loop(1, steps + 1, p_wait, 0)

    def h_rows(to):
        return pl.ds(pl.multiple_of(to * owned, 16), owned)

    def c_copy(level_z):
        return pltpu.make_async_remote_copy(
            src_ref=hs.at[h_rows(level_z * CROSS + 1 - x), :],
            dst_ref=hx.at[level_z],
            send_sem=c_send.at[level_z],
            recv_sem=c_recv.at[level_z],
            device_id=across,
            device_id_type=MESH,
        )

    def h_copy(to, frm):
        return pltpu.make_async_remote_copy(
            src_ref=hq.at[to],
            dst_ref=hr.at[frm],
            send_sem=h_send.at[to],
            recv_sem=h_recv.at[frm],
            device_id=(g, to * CROSS + x, t),
            device_id_type=MESH,
        )

    group = members // 2
    wide_rows = group * owned

    def h_step(k, carry):
        n = (s // group + 1 + k) % 2
        lanes = pl.ds(pl.multiple_of(n * wide_rows, 128), wide_rows)
        total = jnp.zeros((wide_rows, pair_rows), jnp.float32)
        for shard in range(chain):
            total = total + lax.dot_general(
                pb[shard, :, lanes],
                ob[shard * head_rows : (shard + 1) * head_rows, :],
                (((0,), (0,)), ((), ())),
                preferred_element_type=jnp.float32,
            )
        hs[lanes, :] = total.astype(jnp.bfloat16)
        for u in range(group // CROSS):
            c_copy(n * (group // CROSS) + u).start()
        return carry

    lax.fori_loop(0, 2, h_step, 0)

    def h_sum(to):
        c_copy(to).wait_recv()
        mine = hs[h_rows(to * CROSS + x), :].astype(jnp.float32)
        return (mine + hx[to].astype(jnp.float32)).astype(jnp.bfloat16)

    def h_pass(k, carry):
        to = order(steps - k)
        hq[to] = h_sum(to)
        h_copy(to, z).start()
        return carry

    lax.fori_loop(0, steps, h_pass, 0)
    hr[z] = h_sum(z)

    own_x.wait()

    def x_wait(k, carry):
        x_copy(s, peer(k)).wait_recv()
        return carry

    lax.fori_loop(1, members, x_wait, 0)
    for m in range(members):
        xp[:, m * own_rows : (m + 1) * own_rows] = xr[m].astype(jnp.float32)
    xp[:, length:] = jnp.zeros((owned, span), jnp.float32)

    columns = cols.at[1]
    cols[0] = jnp.zeros((128, 128), jnp.float32)
    cols[0, 0:3, 0:owned] = taps[...]
    cols[0, 3:4, 0:owned] = level[...].astype(jnp.float32)
    cols[1] = jnp.transpose(cols[0])
    sums[...] = jnp.zeros((128, 128), jnp.float32)

    def h_wait(j, carry):
        h_copy(z, order(j)).wait_recv()
        return carry

    lax.fori_loop(1, steps + 1, h_wait, 0)

    padded = length + span
    norm = 1.0 / math.sqrt(length)

    def conv_rows(i, carry):
        rows = pl.ds(pl.multiple_of(i * 16, 16), 16)
        lev = columns[rows, 3:4]
        tap = columns[rows, 0:3]

        def pick(value, sign):
            result = None
            for k in range(DILATION_COUNT):
                reach = BASE_DILATION * 2**k
                moved = pltpu.roll(value, reach if sign < 0 else padded - reach, 1)[:, :length]
                result = moved if result is None else jnp.where(lev == float(k), moved, result)
            return result

        wide = xp[rows, :]
        minus = pick(wide, -1)
        plus = pick(wide, 1)
        center = wide[:, :length]
        pre_act = tap[:, 0:1] * minus + tap[:, 1:2] * center + tap[:, 2:3] * plus
        hidden = jnp.concatenate([hr[m, rows, :] for m in range(chain)], axis=1)
        pre_grad = hidden.astype(jnp.float32) * gelu_slope(pre_act)
        sums[rows, 0:1] = jnp.sum(pre_grad * minus, axis=1, keepdims=True) * norm
        sums[rows, 1:2] = jnp.sum(pre_grad * center, axis=1, keepdims=True) * norm
        sums[rows, 2:3] = jnp.sum(pre_grad * plus, axis=1, keepdims=True) * norm
        spread_wide = jnp.concatenate([pre_grad, jnp.zeros((16, span), jnp.float32)], axis=1)
        part = (
            tap[:, 0:1] * pick(spread_wide, 1)
            + tap[:, 1:2] * pre_grad
            + tap[:, 2:3] * pick(spread_wide, -1)
        ).astype(jnp.bfloat16)
        for m in range(members):
            cb[m, rows, :] = part[:, m * own_rows : (m + 1) * own_rows]
        return carry

    back = owned // BACK_PARTS

    def r_copy(to, frm, c):
        rows = pl.ds(pl.multiple_of(c * back, 16), back)
        return pltpu.make_async_remote_copy(
            src_ref=cb.at[to, rows, :],
            dst_ref=rb.at[frm, rows, :],
            send_sem=r_send.at[to, c],
            recv_sem=r_recv.at[frm, c],
            device_id=(g, to, t),
            device_id_type=MESH,
        )

    def conv_part(c, carry):
        lax.fori_loop(c * (back // 16), (c + 1) * (back // 16), conv_rows, 0)

        def r_start(k, inner):
            r_copy(peer(k), s, c).start()
            return inner

        lax.fori_loop(1, members, r_start, 0)
        return carry

    lax.fori_loop(0, BACK_PARTS, conv_part, 0)
    rb[s] = cb[s]
    for q in range(blocks_kept):
        o_copy(q).wait_recv()

    def r_wait(k, carry):
        for c in range(BACK_PARTS):
            r_copy(s, peer(k), c).wait_recv()
        return carry

    lax.fori_loop(1, members, r_wait, 0)

    per = head_rows // owned
    for q in range(blocks_kept):
        for u in range(per):
            mine = (CROSS * q + x) * per + u
            src = pl.ds(pl.multiple_of((t * blocks_kept + q) * head_rows + u * owned, 16), owned)
            here = jnp.where(
                x == 0, ob[src, 0:own_rows].astype(jnp.float32), ob[src, own_rows:].astype(jnp.float32)
            )
            out[pl.ds(pl.multiple_of(mine * owned, 16), owned), :] = (
                here + rb[mine].astype(jnp.float32)
            ).astype(jnp.bfloat16)
            other = (CROSS * q + 1 - x) * per + u
            there = ox[q, u * owned : (u + 1) * owned, :].astype(jnp.float32)
            out[pl.ds(pl.multiple_of(other * owned, 16), owned), :] = (
                there + rb[other].astype(jnp.float32)
            ).astype(jnp.bfloat16)

    tg[...] = jnp.transpose(sums[...])[0:3, 0:owned]

    def w_done(shard, carry):
        def one(c, inner):
            block = wb.at[w_rows(shard, c, g), :]

            @pl.when((shard <= z) & has_up)
            def _():
                w_hop(shard, c, block, z, 0).wait_send()

            @pl.when((shard >= z) & has_down)
            def _():
                w_hop(shard, c, block, z, 1).wait_send()

            @pl.when(shard != z)
            def _():
                w_swap(shard, c, g).wait_send()

            return inner

        lax.fori_loop(0, PARTS, one, 0)
        for c in range(P_PARTS):
            pblock = pb.at[shard, p_rows(c, g), :]

            @pl.when((shard <= z) & has_up)
            def _():
                p_hop(shard, c, pblock, z, 0).wait_send()

            @pl.when((shard >= z) & has_down)
            def _():
                p_hop(shard, c, pblock, z, 1).wait_send()

            @pl.when(shard != z)
            def _():
                p_swap(shard, c, g).wait_send()

        for xs in range(CROSS):
            g_copy(shard, xs).wait_send()
        c_copy(shard).wait_send()

        @pl.when(shard != z)
        def _():
            h_copy(shard, z).wait_send()

        return carry

    lax.fori_loop(0, chain, w_done, 0)

    for c in range(ADJ_PARTS):
        a_copy(c).wait_send()
    for q in range(blocks_kept):
        o_copy(q).wait_send()

    def done(k, carry):
        x_copy(peer(k), s).wait_send()
        for c in range(BACK_PARTS):
            r_copy(peer(k), s, c).wait_send()
        return carry

    lax.fori_loop(1, members, done, 0)


def fused(
    chain,
    section_input,
    conv_taps,
    dilation_level,
    pointwise_matrix,
    head_weight,
    pred_error,
    tail_mask,
    track_scale,
):
    own, own_rows = section_input.shape
    members = chain * CROSS
    owned = own // members
    head_rows, tracks = head_weight.shape
    pair_rows = CROSS * own_rows
    length = members * own_rows
    span = BASE_DILATION * 2 ** (DILATION_COUNT - 1)
    cols = pointwise_matrix.shape[1]
    bf16, f32 = jnp.bfloat16, jnp.float32
    dma = pltpu.SemaphoreType.DMA
    anywhere = pl.BlockSpec(memory_space=pltpu.HBM)
    vmem = pl.BlockSpec(memory_space=pltpu.VMEM)
    input_grad, taps_grad = (
        pl.pallas_call(
            functools.partial(fused_kernel, chain),
            out_shape=(
                jax.ShapeDtypeStruct((own, own_rows), bf16),
                jax.ShapeDtypeStruct((3, owned), f32),
            ),
            in_specs=[anywhere, vmem, vmem, anywhere, anywhere, anywhere, anywhere, vmem],
            out_specs=(vmem, vmem),
            scratch_shapes=[
                pltpu.VMEM((chain * head_rows, tracks), bf16),
                pltpu.VMEM((CROSS, tracks, own_rows), bf16),
                pltpu.VMEM((tracks, own_rows), bf16),
                pltpu.VMEM((tracks, own_rows), jnp.int32),
                pltpu.VMEM((chain, cols, own), bf16),
                pltpu.VMEM((CROSS, chain * head_rows, own_rows), f32),
                pltpu.VMEM((CROSS, chain * head_rows, own_rows), f32),
                pltpu.VMEM((chain * head_rows, pair_rows), bf16),
                pltpu.VMEM((chain // 2, head_rows, own_rows), bf16),
                pltpu.VMEM((own, pair_rows), bf16),
                pltpu.VMEM((chain, owned, pair_rows), bf16),
                pltpu.VMEM((members, owned, own_rows), bf16),
                pltpu.VMEM((owned, length + span), f32),
                pltpu.VMEM((chain, owned, pair_rows), bf16),
                pltpu.VMEM((chain, owned, pair_rows), bf16),
                pltpu.VMEM((members, owned, own_rows), bf16),
                pltpu.VMEM((members, owned, own_rows), bf16),
                pltpu.VMEM((2, 128, 128), f32),
                pltpu.VMEM((128, 128), f32),
                dma((3 + 2 * ADJ_PARTS,)),
                dma((2, chain * PARTS)),
                dma((chain * PARTS,)),
                dma((chain * PARTS,)),
                dma((chain * PARTS,)),
                dma((2, chain * P_PARTS)),
                dma((chain * P_PARTS,)),
                dma((chain * P_PARTS,)),
                dma((chain * P_PARTS,)),
                dma((ADJ_PARTS,)),
                dma((ADJ_PARTS,)),
                dma((chain, CROSS)),
                dma((chain, CROSS)),
                dma((chain // 2,)),
                dma((chain // 2,)),
                dma((members,)),
                dma((members,)),
                dma((chain,)),
                dma((chain,)),
                dma((chain,)),
                dma((chain,)),
                dma((members, BACK_PARTS)),
                dma((members, BACK_PARTS)),
            ],
            compiler_params=pltpu.CompilerParams(
                collective_id=0, has_side_effects=True, vmem_limit_bytes=63 * 1024 * 1024
            ),
            name="fused_section",
        )(
            section_input,
            conv_taps.T,
            dilation_level[None, :],
            pointwise_matrix.T,
            head_weight,
            pred_error.T,
            tail_mask.T,
            track_scale,
        )
    )
    return input_grad, taps_grad.T


def local_or_fused(sizes, *args):
    section_input, head_weight, pred_error = args[0], args[4], args[5]
    seq = sizes["seq"]
    fits = (
        sizes["groups"] == 2
        and sizes["track"] == 2
        and seq == 8
        and head_weight.shape[0] % (2 * PARTS * 16) == 0
        and section_input.shape[0] % (seq * 16) == 0
        and section_input.shape[1] % 128 == 0
        and pred_error.shape[1] % 16 == 0
        and pred_error.shape[1] >= 128 * ADJ_PARTS
        and args[3].shape[1] % (2 * P_PARTS * 16) == 0
        and section_input.shape[0] % 256 == 0
        and section_input.shape[0] // seq <= 128
        and section_input.shape[0] // seq % (BACK_PARTS * 16) == 0
        and head_weight.shape[0] % (section_input.shape[0] // seq) == 0
    )
    if fits:
        return fused(seq // CROSS, *args)
    return local(*args)


def solution(mesh):
    in_specs = (
        P("track", ("groups", "seq")),
        P(("track", "seq"), None),
        P(("track", "seq")),
        P("track", "seq"),
        P("seq", "track"),
        P(("groups", "seq"), "track"),
        P(("groups", "seq"), "track"),
        P("track"),
    )
    sizes = dict(mesh.shape)
    body = functools.partial(local_or_fused, sizes)
    out_specs = (P("track", ("groups", "seq")), P(("groups", "track", "seq"), None))
    return jax.shard_map(body, mesh=mesh, in_specs=in_specs, out_specs=out_specs, check_vma=False)
```

```python
import functools
import math

import jax
import jax.numpy as jnp
from jax import lax
from jax.experimental import pallas as pl
from jax.experimental.pallas import tpu as pltpu
from jax.sharding import PartitionSpec as P

DILATION_COUNT = 5
BASE_DILATION = 32


root_half = 0.7071067811865476
norm_const = 0.3989422804014327


def gelu_slope(value):
    return 0.5 * (1.0 + jax.scipy.special.erf(value * root_half)) + value * norm_const * jnp.exp(
        -0.5 * value * value
    )


def taps_at(buffer, onehot, margin, sign):
    width_own = buffer.shape[1] - 2 * margin
    result = jnp.zeros((buffer.shape[0], width_own), jnp.float32)
    for level_index in range(onehot.shape[1]):
        receptive_span = BASE_DILATION * 2**level_index
        begin = margin + sign * receptive_span
        result = (
            result + onehot[:, level_index : level_index + 1] * buffer[:, begin : begin + width_own]
        )
    return result


def spread(values, onehot, margin, sign):
    result = jnp.zeros((values.shape[0], values.shape[1] + 2 * margin), jnp.float32)
    for level_index in range(onehot.shape[1]):
        receptive_span = BASE_DILATION * 2**level_index
        placed = onehot[:, level_index : level_index + 1] * values
        result = result + jnp.pad(
            placed, ((0, 0), (margin + sign * receptive_span, margin - sign * receptive_span))
        )
    return result


def channel_grads(buffer, hidden_grad, taps, onehot, margin):
    width_own = buffer.shape[1] - 2 * margin
    minus_side = taps_at(buffer, onehot, margin, -1)
    center = buffer[:, margin : margin + width_own]
    plus_side = taps_at(buffer, onehot, margin, 1)
    pre_act = taps[:, 0:1] * minus_side + taps[:, 1:2] * center + taps[:, 2:3] * plus_side
    pre_grad = hidden_grad.astype(jnp.float32) * gelu_slope(pre_act)
    taps_part = jnp.stack(
        [
            jnp.sum(pre_grad * minus_side, axis=1),
            jnp.sum(pre_grad * center, axis=1),
            jnp.sum(pre_grad * plus_side, axis=1),
        ],
        axis=1,
    )
    contrib = spread(taps[:, 0:1] * pre_grad, onehot, margin, -1) + spread(
        taps[:, 2:3] * pre_grad, onehot, margin, 1
    )
    contrib = contrib + jnp.pad(taps[:, 1:2] * pre_grad, ((0, 0), (margin, margin)))
    return (contrib, taps_part)


def local(
    section_input,
    conv_taps,
    dilation_level,
    pointwise_matrix,
    head_weight,
    pred_error,
    tail_mask,
    track_scale,
):
    own_channels = section_input.shape[0]
    own_rows = section_input.shape[1]
    adjoint = (
        tail_mask.astype(jnp.float32) * track_scale[None, :] * pred_error.astype(jnp.float32)
    ).astype(jnp.bfloat16)
    full_grad = lax.dot_general(
        lax.all_gather(head_weight, "seq", axis=0, tiled=True),
        adjoint,
        (((1,), (1,)), ((), ())),
        preferred_element_type=jnp.float32,
    )
    total = lax.psum(full_grad, "track")
    out_grad_b = total.astype(jnp.bfloat16)
    out_grad = lax.dynamic_slice_in_dim(
        total, lax.axis_index("track") * own_channels, own_channels, 0
    )
    hidden_grad = jnp.dot(
        lax.all_gather(pointwise_matrix, "seq", axis=1, tiled=True),
        out_grad_b,
        preferred_element_type=jnp.float32,
    ).astype(jnp.bfloat16)
    largest_span = BASE_DILATION * 2 ** (DILATION_COUNT - 1)
    scale = 1.0 / math.sqrt(own_rows * lax.axis_size("seq"))
    onehot = (
        dilation_level[:, None] == jnp.arange(DILATION_COUNT, dtype=jnp.int32)[None, :]
    ).astype(jnp.float32)
    owned_input, owned_grad = (
        lax.all_to_all(section_input, "seq", split_axis=0, concat_axis=1, tiled=True),
        lax.all_to_all(hidden_grad, "seq", split_axis=0, concat_axis=1, tiled=True),
    )
    padded = jnp.pad(owned_input.astype(jnp.float32), ((0, 0), (largest_span, largest_span)))
    contrib, taps_part = channel_grads(padded, owned_grad, conv_taps, onehot, largest_span)
    window = contrib[:, largest_span : largest_span + owned_input.shape[1]]
    conv_part = lax.all_to_all(window, "seq", split_axis=1, concat_axis=0, tiled=True)
    taps_grad = taps_part * scale
    input_grad = (out_grad + conv_part).astype(jnp.bfloat16)
    return (input_grad, taps_grad)


MESH = pl.DeviceIdType.MESH
CROSS = 2
PARTS = 6
ADJ_PARTS = 4
BACK_PARTS = 3
P_PARTS = 3


def fused_kernel(
    chain,
    sec,
    taps,
    level,
    pw,
    hw,
    err,
    mask,
    scale,
    out,
    tg,
    wb,
    ab,
    ev,
    mv,
    pb,
    gp,
    gr,
    ob,
    ox,
    hs,
    hr,
    xr,
    xp,
    hx,
    hq,
    cb,
    rb,
    cols,
    sums,
    ld_sem,
    w_send,
    w_recv,
    wy_send,
    wy_recv,
    p_send,
    p_recv,
    py_send,
    py_recv,
    a_send,
    a_recv,
    g_send,
    g_recv,
    o_send,
    o_recv,
    x_send,
    x_recv,
    c_send,
    c_recv,
    h_send,
    h_recv,
    r_send,
    r_recv,
):
    g = lax.axis_index("groups")
    s = lax.axis_index("seq")
    t = lax.axis_index("track")
    members = chain * CROSS
    z = s // CROSS
    x = s % CROSS
    head_rows = hw.shape[0]
    half = head_rows // 2
    piece = half // PARTS
    tracks, own_rows = err.shape
    own = sec.shape[0]
    owned = own // members
    phalf = pw.shape[0] // 2
    step = tracks // ADJ_PARTS // 128 * 128
    cuts = [c * step for c in range(ADJ_PARTS)] + [tracks]
    pair_rows = CROSS * own_rows
    length = members * own_rows
    span = xp.shape[1] - length

    sibling = (g, s, 1 - t)
    twin = (1 - g, s, t)
    across = (g, z * CROSS + 1 - x, t)

    def peer(k):
        return lax.rem(s + k, members)

    barrier = pltpu.get_barrier_semaphore()

    def greet(k, carry):
        pl.semaphore_signal(barrier, inc=1, device_id=(g, peer(k), t), device_id_type=MESH)
        return carry

    lax.fori_loop(1, members, greet, 0)
    pl.semaphore_signal(barrier, inc=1, device_id=sibling, device_id_type=MESH)
    pl.semaphore_signal(barrier, inc=1, device_id=twin, device_id_type=MESH)

    own_w = pltpu.make_async_copy(
        hw, wb.at[pl.ds(pl.multiple_of(z * head_rows, 16), head_rows), :], ld_sem.at[0]
    )
    own_p = pltpu.make_async_copy(pw, pb.at[z], ld_sem.at[1])
    own_x = pltpu.make_async_copy(sec.at[pl.ds(pl.multiple_of(s * owned, 16), owned), :], xr.at[s], ld_sem.at[2])
    loads = []
    for c in range(ADJ_PARTS):
        rows = pl.ds(cuts[c], cuts[c + 1] - cuts[c])
        loads.append(
            (
                pltpu.make_async_copy(err.at[rows, :], ev.at[rows, :], ld_sem.at[3 + 2 * c]),
                pltpu.make_async_copy(mask.at[rows, :], mv.at[rows, :], ld_sem.at[4 + 2 * c]),
            )
        )
    for first, second in loads:
        first.start()
        second.start()
    own_w.start()
    own_p.start()
    own_x.start()
    pl.semaphore_wait(barrier, members - 1 + 2)

    def w_rows(shard, c, which):
        return pl.ds(pl.multiple_of(shard * head_rows + which * half + c * piece, 16), piece)

    def w_hop(shard, c, src, toward, direction):
        slot = shard * PARTS + c
        return pltpu.make_async_remote_copy(
            src_ref=src,
            dst_ref=wb.at[w_rows(shard, c, g), :],
            send_sem=w_send.at[direction, slot],
            recv_sem=w_recv.at[slot],
            device_id=(g, toward * CROSS + x, t),
            device_id_type=MESH,
        )

    def w_swap(shard, c, which):
        slot = shard * PARTS + c
        block = wb.at[w_rows(shard, c, which), :]
        return pltpu.make_async_remote_copy(
            src_ref=block,
            dst_ref=block,
            send_sem=wy_send.at[slot],
            recv_sem=wy_recv.at[slot],
            device_id=twin,
            device_id_type=MESH,
        )

    p_piece = phalf // P_PARTS

    def p_rows(c, which):
        return pl.ds(pl.multiple_of(which * phalf + c * p_piece, 16), p_piece)

    def p_hop(shard, c, src, toward, direction):
        slot = shard * P_PARTS + c
        return pltpu.make_async_remote_copy(
            src_ref=src,
            dst_ref=pb.at[shard, p_rows(c, g), :],
            send_sem=p_send.at[direction, slot],
            recv_sem=p_recv.at[slot],
            device_id=(g, toward * CROSS + x, t),
            device_id_type=MESH,
        )

    def p_swap(shard, c, which):
        slot = shard * P_PARTS + c
        block = pb.at[shard, p_rows(c, which), :]
        return pltpu.make_async_remote_copy(
            src_ref=block,
            dst_ref=block,
            send_sem=py_send.at[slot],
            recv_sem=py_recv.at[slot],
            device_id=twin,
            device_id_type=MESH,
        )

    has_up = z < chain - 1
    has_down = z > 0

    def own_piece(c):
        return hw.at[pl.ds(pl.multiple_of(g * half + c * piece, 16), piece), :]


    @pl.when(has_up)
    def _():
        for c in range(PARTS):
            w_hop(z, c, own_piece(c), z + 1, 0).start()

    @pl.when(has_down)
    def _():
        for c in range(PARTS):
            w_hop(z, c, own_piece(c), z - 1, 1).start()

    def a_copy(c):
        rows = pl.ds(cuts[c], cuts[c + 1] - cuts[c])
        block = ab.at[x, rows, :]
        return pltpu.make_async_remote_copy(
            src_ref=block,
            dst_ref=block,
            send_sem=a_send.at[c],
            recv_sem=a_recv.at[c],
            device_id=across,
            device_id_type=MESH,
        )

    for c in range(ADJ_PARTS):
        loads[c][0].wait()
        loads[c][1].wait()

        def fill(begin, count):
            rows = pl.ds(begin, count)
            line = scale[rows].reshape(1, count)
            if count < 128:
                line = jnp.concatenate([line, jnp.zeros((1, 128 - count), jnp.float32)], axis=1)
            column = jnp.transpose(jnp.broadcast_to(line, (128, 128)))[:count]
            column = jnp.concatenate([column] * (own_rows // 128), axis=1)
            value = mv[rows, :].astype(jnp.float32) * column * ev[rows, :].astype(jnp.float32)
            ab[x, rows, :] = value.astype(jnp.bfloat16)

        def fill_step(i, carry):
            fill(pl.multiple_of(cuts[c] + i * 128, 128), 128)
            return carry

        whole, rest = divmod(cuts[c + 1] - cuts[c], 128)
        lax.fori_loop(0, whole, fill_step, 0)
        if rest:
            fill(cuts[c] + whole * 128, rest)
        a_copy(c).start()

    @pl.when(has_up)
    def _():
        for c in range(P_PARTS):
            p_hop(z, c, pw.at[p_rows(c, g), :], z + 1, 0).start()

    @pl.when(has_down)
    def _():
        for c in range(P_PARTS):
            p_hop(z, c, pw.at[p_rows(c, g), :], z - 1, 1).start()

    def x_copy(to, frm):
        return pltpu.make_async_remote_copy(
            src_ref=sec.at[pl.ds(pl.multiple_of(to * owned, 16), owned), :],
            dst_ref=xr.at[frm],
            send_sem=x_send.at[to],
            recv_sem=x_recv.at[frm],
            device_id=(g, to, t),
            device_id_type=MESH,
        )

    def x_start(k, carry):
        x_copy(peer(k), s).start()
        return carry


    below = z
    above = chain - 1 - z
    near = jnp.minimum(below, above)

    def order(j):
        step = (j + 1) // 2
        alternate = jnp.where(j % 2 == 1, z - step, z + step)
        one_sided = jnp.where(above > below, z + (j - near), z - (j - near))
        return jnp.where(j <= 2 * near, alternate, one_sided)

    def g_copy(shard, xs):
        rows = pl.ds(pl.multiple_of(shard * head_rows, 16), head_rows)
        return pltpu.make_async_remote_copy(
            src_ref=gp.at[xs, rows, :],
            dst_ref=gr.at[xs, rows, :],
            send_sem=g_send.at[shard, xs],
            recv_sem=g_recv.at[shard, xs],
            device_id=sibling,
            device_id_type=MESH,
        )

    def head_dot(shard, xs):
        rows = pl.ds(pl.multiple_of(shard * head_rows, 16), head_rows)
        gp[xs, rows, :] = lax.dot_general(
            wb[rows, :],
            ab[xs],
            (((1,), (0,)), ((), ())),
            preferred_element_type=jnp.float32,
        )
        g_copy(shard, xs).start()

    def w_relay(e, carry):
        paired = (near >= 1) & (e < 2 * PARTS)
        j = jnp.where(paired, 1 + e % 2, e // PARTS + 1)
        c = jnp.where(paired, e // 2, e % PARTS)
        shard = order(j)
        block = wb.at[w_rows(shard, c, g), :]
        w_hop(shard, c, block, z, 0).wait_recv()

        @pl.when((shard < z) & has_up)
        def _():
            w_hop(shard, c, block, z + 1, 0).start()

        @pl.when((shard > z) & has_down)
        def _():
            w_hop(shard, c, block, z - 1, 1).start()

        w_swap(shard, c, g).start()
        return carry

    def wait_swaps(shard):
        def one(c, carry):
            w_swap(shard, c, 1 - g).wait_recv()
            return carry

        lax.fori_loop(0, PARTS, one, 0)

    own_w.wait()
    head_dot(z, x)
    steps = chain - 1
    lax.fori_loop(0, (steps - 1) * PARTS, w_relay, 0)

    def early(j, carry):
        shard = order(j)
        wait_swaps(shard)
        head_dot(shard, x)
        return carry

    lax.fori_loop(1, steps - 1, early, 0)
    lax.fori_loop((steps - 1) * PARTS, steps * PARTS, w_relay, 0)
    lax.fori_loop(jnp.maximum(steps - 1, 1), steps, early, 0)

    for c in range(ADJ_PARTS):
        block = ab.at[1 - x, pl.ds(cuts[c], cuts[c + 1] - cuts[c]), :]
        pltpu.make_async_remote_copy(
            src_ref=block,
            dst_ref=block,
            send_sem=a_send.at[c],
            recv_sem=a_recv.at[c],
            device_id=across,
            device_id_type=MESH,
        ).wait_recv()

    def late(j, carry):
        head_dot(jnp.where(j == 0, z, order(jnp.maximum(j, 1))), 1 - x)
        return carry

    lax.fori_loop(0, steps, late, 0)

    def p_relay(e, carry):
        shard = order(e // P_PARTS + 1)
        c = e % P_PARTS
        block = pb.at[shard, p_rows(c, g), :]
        p_hop(shard, c, block, z, 0).wait_recv()

        @pl.when((shard < z) & has_up)
        def _():
            p_hop(shard, c, block, z + 1, 0).start()

        @pl.when((shard > z) & has_down)
        def _():
            p_hop(shard, c, block, z - 1, 1).start()

        p_swap(shard, c, g).start()
        return carry

    lax.fori_loop(0, (steps - 1) * P_PARTS, p_relay, 0)
    last = order(steps)
    wait_swaps(last)
    head_dot(last, x)
    head_dot(last, 1 - x)
    lax.fori_loop(1, members, x_start, 0)
    lax.fori_loop((steps - 1) * P_PARTS, steps * P_PARTS, p_relay, 0)

    def core_sum(j, carry):
        shard = jnp.where(j == 0, z, order(jnp.maximum(j, 1)))
        rows = pl.ds(pl.multiple_of(shard * head_rows, 16), head_rows)
        for xs in range(CROSS):
            g_copy(shard, xs).wait_recv()
            ob[rows, xs * own_rows : (xs + 1) * own_rows] = (gp[xs, rows, :] + gr[xs, rows, :]).astype(
                jnp.bfloat16
            )
        return carry

    lax.fori_loop(0, chain, core_sum, 0)

    blocks_kept = chain // 2

    def o_copy(q):
        return pltpu.make_async_remote_copy(
            src_ref=ob.at[
                pl.ds(pl.multiple_of((t * blocks_kept + q) * head_rows, 16), head_rows),
                pl.ds(pl.multiple_of((1 - x) * own_rows, 128), own_rows),
            ],
            dst_ref=ox.at[q],
            send_sem=o_send.at[q],
            recv_sem=o_recv.at[q],
            device_id=across,
            device_id_type=MESH,
        )

    own_p.wait()

    def p_wait(j, carry):
        for c in range(P_PARTS):
            p_swap(order(j), c, 1 - g).wait_recv()
        return carry

    lax.fori_loop(1, steps + 1, p_wait, 0)

    def h_rows(to):
        return pl.ds(pl.multiple_of(to * owned, 16), owned)

    def c_copy(level_z):
        return pltpu.make_async_remote_copy(
            src_ref=hs.at[h_rows(level_z * CROSS + 1 - x), :],
            dst_ref=hx.at[level_z],
            send_sem=c_send.at[level_z],
            recv_sem=c_recv.at[level_z],
            device_id=across,
            device_id_type=MESH,
        )

    def h_copy(to, frm):
        return pltpu.make_async_remote_copy(
            src_ref=hq.at[to],
            dst_ref=hr.at[frm],
            send_sem=h_send.at[to],
            recv_sem=h_recv.at[frm],
            device_id=(g, to * CROSS + x, t),
            device_id_type=MESH,
        )

    group = members // 2
    wide_rows = group * owned

    def h_step(k, carry):
        n = (s // group + 1 + k) % 2
        lanes = pl.ds(pl.multiple_of(n * wide_rows, 128), wide_rows)
        total = jnp.zeros((wide_rows, pair_rows), jnp.float32)
        for shard in range(chain):
            total = total + lax.dot_general(
                pb[shard, :, lanes],
                ob[shard * head_rows : (shard + 1) * head_rows, :],
                (((0,), (0,)), ((), ())),
                preferred_element_type=jnp.float32,
            )
        hs[lanes, :] = total.astype(jnp.bfloat16)
        for u in range(group // CROSS):
            c_copy(n * (group // CROSS) + u).start()
        return carry

    lax.fori_loop(0, 2, h_step, 0)

    for q in range(blocks_kept):
        o_copy(q).start()

    def h_sum(to):
        c_copy(to).wait_recv()
        mine = hs[h_rows(to * CROSS + x), :].astype(jnp.float32)
        return (mine + hx[to].astype(jnp.float32)).astype(jnp.bfloat16)

    def h_pass(k, carry):
        to = order(steps - k)
        hq[to] = h_sum(to)
        h_copy(to, z).start()
        return carry

    lax.fori_loop(0, steps, h_pass, 0)
    hr[z] = h_sum(z)

    own_x.wait()

    def x_wait(k, carry):
        x_copy(s, peer(k)).wait_recv()
        return carry

    lax.fori_loop(1, members, x_wait, 0)
    for m in range(members):
        xp[:, m * own_rows : (m + 1) * own_rows] = xr[m].astype(jnp.float32)
    xp[:, length:] = jnp.zeros((owned, span), jnp.float32)

    columns = cols.at[1]
    cols[0] = jnp.zeros((128, 128), jnp.float32)
    cols[0, 0:3, 0:owned] = taps[...]
    cols[0, 3:4, 0:owned] = level[...].astype(jnp.float32)
    cols[1] = jnp.transpose(cols[0])
    sums[...] = jnp.zeros((128, 128), jnp.float32)

    def h_wait(j, carry):
        h_copy(z, order(j)).wait_recv()
        return carry

    lax.fori_loop(1, steps + 1, h_wait, 0)

    padded = length + span
    norm = 1.0 / math.sqrt(length)

    def conv_rows(i, carry):
        rows = pl.ds(pl.multiple_of(i * 16, 16), 16)
        lev = columns[rows, 3:4]
        tap = columns[rows, 0:3]

        def pick(value, sign):
            result = None
            for k in range(DILATION_COUNT):
                reach = BASE_DILATION * 2**k
                moved = pltpu.roll(value, reach if sign < 0 else padded - reach, 1)[:, :length]
                result = moved if result is None else jnp.where(lev == float(k), moved, result)
            return result

        wide = xp[rows, :]
        minus = pick(wide, -1)
        plus = pick(wide, 1)
        center = wide[:, :length]
        pre_act = tap[:, 0:1] * minus + tap[:, 1:2] * center + tap[:, 2:3] * plus
        hidden = jnp.concatenate([hr[m, rows, :] for m in range(chain)], axis=1)
        pre_grad = hidden.astype(jnp.float32) * gelu_slope(pre_act)
        sums[rows, 0:1] = jnp.sum(pre_grad * minus, axis=1, keepdims=True) * norm
        sums[rows, 1:2] = jnp.sum(pre_grad * center, axis=1, keepdims=True) * norm
        sums[rows, 2:3] = jnp.sum(pre_grad * plus, axis=1, keepdims=True) * norm
        spread_wide = jnp.concatenate([pre_grad, jnp.zeros((16, span), jnp.float32)], axis=1)
        part = (
            tap[:, 0:1] * pick(spread_wide, 1)
            + tap[:, 1:2] * pre_grad
            + tap[:, 2:3] * pick(spread_wide, -1)
        ).astype(jnp.bfloat16)
        for m in range(members):
            cb[m, rows, :] = part[:, m * own_rows : (m + 1) * own_rows]
        return carry

    back = owned // BACK_PARTS

    def r_copy(to, frm, c):
        rows = pl.ds(pl.multiple_of(c * back, 16), back)
        return pltpu.make_async_remote_copy(
            src_ref=cb.at[to, rows, :],
            dst_ref=rb.at[frm, rows, :],
            send_sem=r_send.at[to, c],
            recv_sem=r_recv.at[frm, c],
            device_id=(g, to, t),
            device_id_type=MESH,
        )

    def conv_part(c, carry):
        lax.fori_loop(c * (back // 16), (c + 1) * (back // 16), conv_rows, 0)

        def r_start(k, inner):
            r_copy(peer(k), s, c).start()
            return inner

        lax.fori_loop(1, members, r_start, 0)
        return carry

    lax.fori_loop(0, BACK_PARTS, conv_part, 0)
    rb[s] = cb[s]
    for q in range(blocks_kept):
        o_copy(q).wait_recv()

    def r_wait(k, carry):
        for c in range(BACK_PARTS):
            r_copy(s, peer(k), c).wait_recv()
        return carry

    lax.fori_loop(1, members, r_wait, 0)

    per = head_rows // owned
    for q in range(blocks_kept):
        for u in range(per):
            mine = (CROSS * q + x) * per + u
            src = pl.ds(pl.multiple_of((t * blocks_kept + q) * head_rows + u * owned, 16), owned)
            here = jnp.where(
                x == 0, ob[src, 0:own_rows].astype(jnp.float32), ob[src, own_rows:].astype(jnp.float32)
            )
            out[pl.ds(pl.multiple_of(mine * owned, 16), owned), :] = (
                here + rb[mine].astype(jnp.float32)
            ).astype(jnp.bfloat16)
            other = (CROSS * q + 1 - x) * per + u
            there = ox[q, u * owned : (u + 1) * owned, :].astype(jnp.float32)
            out[pl.ds(pl.multiple_of(other * owned, 16), owned), :] = (
                there + rb[other].astype(jnp.float32)
            ).astype(jnp.bfloat16)

    tg[...] = jnp.transpose(sums[...])[0:3, 0:owned]

    def w_done(shard, carry):
        def one(c, inner):
            block = wb.at[w_rows(shard, c, g), :]

            @pl.when((shard <= z) & has_up)
            def _():
                w_hop(shard, c, block, z, 0).wait_send()

            @pl.when((shard >= z) & has_down)
            def _():
                w_hop(shard, c, block, z, 1).wait_send()

            @pl.when(shard != z)
            def _():
                w_swap(shard, c, g).wait_send()

            return inner

        lax.fori_loop(0, PARTS, one, 0)
        for c in range(P_PARTS):
            pblock = pb.at[shard, p_rows(c, g), :]

            @pl.when((shard <= z) & has_up)
            def _():
                p_hop(shard, c, pblock, z, 0).wait_send()

            @pl.when((shard >= z) & has_down)
            def _():
                p_hop(shard, c, pblock, z, 1).wait_send()

            @pl.when(shard != z)
            def _():
                p_swap(shard, c, g).wait_send()

        for xs in range(CROSS):
            g_copy(shard, xs).wait_send()
        c_copy(shard).wait_send()

        @pl.when(shard != z)
        def _():
            h_copy(shard, z).wait_send()

        return carry

    lax.fori_loop(0, chain, w_done, 0)

    for c in range(ADJ_PARTS):
        a_copy(c).wait_send()
    for q in range(blocks_kept):
        o_copy(q).wait_send()

    def done(k, carry):
        x_copy(peer(k), s).wait_send()
        for c in range(BACK_PARTS):
            r_copy(peer(k), s, c).wait_send()
        return carry

    lax.fori_loop(1, members, done, 0)


def fused(
    chain,
    section_input,
    conv_taps,
    dilation_level,
    pointwise_matrix,
    head_weight,
    pred_error,
    tail_mask,
    track_scale,
):
    own, own_rows = section_input.shape
    members = chain * CROSS
    owned = own // members
    head_rows, tracks = head_weight.shape
    pair_rows = CROSS * own_rows
    length = members * own_rows
    span = BASE_DILATION * 2 ** (DILATION_COUNT - 1)
    cols = pointwise_matrix.shape[1]
    bf16, f32 = jnp.bfloat16, jnp.float32
    dma = pltpu.SemaphoreType.DMA
    anywhere = pl.BlockSpec(memory_space=pltpu.HBM)
    vmem = pl.BlockSpec(memory_space=pltpu.VMEM)
    input_grad, taps_grad = (
        pl.pallas_call(
            functools.partial(fused_kernel, chain),
            out_shape=(
                jax.ShapeDtypeStruct((own, own_rows), bf16),
                jax.ShapeDtypeStruct((3, owned), f32),
            ),
            in_specs=[anywhere, vmem, vmem, anywhere, anywhere, anywhere, anywhere, vmem],
            out_specs=(vmem, vmem),
            scratch_shapes=[
                pltpu.VMEM((chain * head_rows, tracks), bf16),
                pltpu.VMEM((CROSS, tracks, own_rows), bf16),
                pltpu.VMEM((tracks, own_rows), bf16),
                pltpu.VMEM((tracks, own_rows), jnp.int32),
                pltpu.VMEM((chain, cols, own), bf16),
                pltpu.VMEM((CROSS, chain * head_rows, own_rows), f32),
                pltpu.VMEM((CROSS, chain * head_rows, own_rows), f32),
                pltpu.VMEM((chain * head_rows, pair_rows), bf16),
                pltpu.VMEM((chain // 2, head_rows, own_rows), bf16),
                pltpu.VMEM((own, pair_rows), bf16),
                pltpu.VMEM((chain, owned, pair_rows), bf16),
                pltpu.VMEM((members, owned, own_rows), bf16),
                pltpu.VMEM((owned, length + span), f32),
                pltpu.VMEM((chain, owned, pair_rows), bf16),
                pltpu.VMEM((chain, owned, pair_rows), bf16),
                pltpu.VMEM((members, owned, own_rows), bf16),
                pltpu.VMEM((members, owned, own_rows), bf16),
                pltpu.VMEM((2, 128, 128), f32),
                pltpu.VMEM((128, 128), f32),
                dma((3 + 2 * ADJ_PARTS,)),
                dma((2, chain * PARTS)),
                dma((chain * PARTS,)),
                dma((chain * PARTS,)),
                dma((chain * PARTS,)),
                dma((2, chain * P_PARTS)),
                dma((chain * P_PARTS,)),
                dma((chain * P_PARTS,)),
                dma((chain * P_PARTS,)),
                dma((ADJ_PARTS,)),
                dma((ADJ_PARTS,)),
                dma((chain, CROSS)),
                dma((chain, CROSS)),
                dma((chain // 2,)),
                dma((chain // 2,)),
                dma((members,)),
                dma((members,)),
                dma((chain,)),
                dma((chain,)),
                dma((chain,)),
                dma((chain,)),
                dma((members, BACK_PARTS)),
                dma((members, BACK_PARTS)),
            ],
            compiler_params=pltpu.CompilerParams(
                collective_id=0, has_side_effects=True, vmem_limit_bytes=63 * 1024 * 1024
            ),
            name="fused_section",
        )(
            section_input,
            conv_taps.T,
            dilation_level[None, :],
            pointwise_matrix.T,
            head_weight,
            pred_error.T,
            tail_mask.T,
            track_scale,
        )
    )
    return input_grad, taps_grad.T


def local_or_fused(sizes, *args):
    section_input, head_weight, pred_error = args[0], args[4], args[5]
    seq = sizes["seq"]
    fits = (
        sizes["groups"] == 2
        and sizes["track"] == 2
        and seq == 8
        and head_weight.shape[0] % (2 * PARTS * 16) == 0
        and section_input.shape[0] % (seq * 16) == 0
        and section_input.shape[1] % 128 == 0
        and pred_error.shape[1] % 16 == 0
        and pred_error.shape[1] >= 128 * ADJ_PARTS
        and args[3].shape[1] % (2 * P_PARTS * 16) == 0
        and section_input.shape[0] % 256 == 0
        and section_input.shape[0] // seq <= 128
        and section_input.shape[0] // seq % (BACK_PARTS * 16) == 0
        and head_weight.shape[0] % (section_input.shape[0] // seq) == 0
    )
    if fits:
        return fused(seq // CROSS, *args)
    return local(*args)


def solution(mesh):
    in_specs = (
        P("track", ("groups", "seq")),
        P(("track", "seq"), None),
        P(("track", "seq")),
        P("track", "seq"),
        P("seq", "track"),
        P(("groups", "seq"), "track"),
        P(("groups", "seq"), "track"),
        P("track"),
    )
    sizes = dict(mesh.shape)
    body = functools.partial(local_or_fused, sizes)
    out_specs = (P("track", ("groups", "seq")), P(("groups", "track", "seq"), None))
    return jax.shard_map(body, mesh=mesh, in_specs=in_specs, out_specs=out_specs, check_vma=False)
```
